32 devices in a mesh: tm: 8 (over z, x), space: 4 (over y, core).
Axes of the slice: x: 2, y: 2, z: 4, core: 2. Of those that a mesh axis runs over, the one named last changes fastest.
Arguments:
- queries: bfloat16 [8, 512, 2048], P('tm', 'space'), may hold values from -180 to 180
- key_vectors: bfloat16 [8, 512, 2048], P('tm', 'space'), may hold values from -6 to 6
- value_vectors: bfloat16 [8, 512, 2048], P('tm', 'space'), may hold values from -96 to 96
- block_lists: int32 [4, 3], replicated, may hold values from 0 to 3, as said below
- step_sizes: float32 [8, 512, 16], P(None, ('space', 'tm')), may hold values from 0.004 to 0.6, as said below
- decay_rates: float32 [16], replicated, may hold values from 0.7 to 1.4
- skip_gains: float32 [16], replicated, may hold values from 0.5 to 1.5
- pre_gain: float32 [2048], replicated, may hold values from 0.25 to 1.75
- state_in_weight: bfloat16 [2048, 64], replicated, may hold values from -0.125 to 0.125
- state_out_weight: bfloat16 [2048, 64], replicated, may hold values from -0.125 to 0.125
- post_gain: float32 [2048], replicated, may hold values from 0.25 to 1.75
Outputs:
- mixed_out: bfloat16 [8, 512, 2048], P('tm', 'space')
The draws below stay inside these ranges and needn't reach their ends.
Inputs may be any that keep to these rules, and one draw needn't show every extreme that they name: `block_lists`: row i lists 3 different key blocks; its first entry is i itself. `step_sizes`: positive step sizes.
All inputs are finite; a program needn't handle non-finite values.
Results may differ from the reference program's by a relative error of at most 0.01.
Values may be sent and summed in bfloat16 or wider, within the bound.
A program may use at most 64 MiB of HBM per device.

```python
import math
from functools import partial
import jax
import jax.numpy as jnp
from jax import lax

SHARED_HEADS = 16
HEAD_DIM = 128
STATE = 64
BLOCK = 128
LATENT_FRAMES = 8
FTOK = 512
NBLK = 4
KSEL = 3
HD = 2048


def paired_states(base_key):
    own_key = jax.random.fold_in(base_key, 17)
    key_q, key_k = jax.random.split(own_key, 2)
    full_shape = (LATENT_FRAMES, FTOK, SHARED_HEADS * HEAD_DIM)
    query_draw = jnp.clip(jax.random.normal(key_q, full_shape, jnp.float32), -6.0, 6.0)
    key_draw = jnp.clip(jax.random.normal(key_k, full_shape, jnp.float32), -6.0, 6.0)
    return (query_draw, key_draw)


def draw_queries(key, part):
    return paired_states(key)[0].astype(jnp.bfloat16)


def draw_key_vectors(key, part):
    return paired_states(key)[1].astype(jnp.bfloat16)


def draw_value_vectors(key, part):
    own_key = jax.random.fold_in(key, 23)
    key_a, key_b, key_c = jax.random.split(own_key, 3)
    full_shape = (LATENT_FRAMES, FTOK, SHARED_HEADS * HEAD_DIM)
    frame_scale = jnp.exp(jax.random.uniform(key_a, (LATENT_FRAMES, 1, 1), jnp.float32, math.log(0.4), math.log(4.0)))
    column_scale = jnp.exp(jax.random.uniform(key_b, (1, 1, SHARED_HEADS * HEAD_DIM), jnp.float32, math.log(0.4), math.log(4.0)))
    core = jnp.clip(jax.random.normal(key_c, full_shape, jnp.float32), -6.0, 6.0)
    return (core * frame_scale * column_scale).astype(jnp.bfloat16)


def draw_block_lists(key, part):
    own_key = jax.random.fold_in(key, 29)
    rank_keys = jax.random.randint(own_key, (NBLK, NBLK), 0, 2 ** 20) * NBLK + jnp.arange(NBLK)[None, :]
    rank_keys = jnp.where(jnp.eye(NBLK, dtype=bool), -1, rank_keys)
    ordering = jnp.argsort(rank_keys, axis=1, stable=True)
    return ordering[:, :KSEL].astype(jnp.int32)


def draw_step_sizes(key, part):
    own_key = jax.random.fold_in(key, 31)
    key_a, key_b, key_c, key_d, random_key_fifth, random_key_sixth = jax.random.split(own_key, 6)
    full_shape = (LATENT_FRAMES, FTOK, SHARED_HEADS)
    fast_count = SHARED_HEADS // 2
    fast_heads = jax.random.permutation(key_a, SHARED_HEADS) < fast_count
    slow_rate = jnp.exp(jax.random.uniform(key_b, (SHARED_HEADS,), jnp.float32, math.log(0.008), math.log(0.02)))
    fast_rate = jnp.exp(jax.random.uniform(key_c, (SHARED_HEADS,), jnp.float32, math.log(0.12), math.log(0.3)))
    baseline_rate = jnp.where(fast_heads, fast_rate, slow_rate)
    jaggedness = jnp.exp(jax.random.uniform(key_d, full_shape, jnp.float32, math.log(0.5), math.log(2.0)))
    spike_frames = jax.random.randint(random_key_fifth, (2, SHARED_HEADS), 0, LATENT_FRAMES)
    spike_mask = jnp.any(jnp.arange(LATENT_FRAMES)[None, :, None] == spike_frames[:, None, :], axis=0)
    spike_length = jax.random.uniform(random_key_sixth, (LATENT_FRAMES, SHARED_HEADS), jnp.float32, 0.3, 0.5)
    return jnp.where(spike_mask[:, None, :], spike_length[:, None, :], baseline_rate * jaggedness)


def normal_values(stream_key, dims, scale, reach, held_as=jnp.bfloat16):
    entries = jax.random.normal(stream_key, dims, jnp.float32) * scale
    return jnp.minimum(jnp.maximum(entries, -reach), reach).astype(held_as)


def setup_inputs(seed: int = 0) -> dict:
    key_list = jax.random.split(jax.random.key(seed), 12)
    return {
        "queries": draw_queries(jax.random.fold_in(key_list[11], 71), 0),
        "key_vectors": draw_key_vectors(jax.random.fold_in(key_list[11], 71), 0),
        "value_vectors": draw_value_vectors(jax.random.fold_in(key_list[11], 71), 0),
        "block_lists": draw_block_lists(jax.random.fold_in(key_list[11], 71), 0),
        "step_sizes": draw_step_sizes(jax.random.fold_in(key_list[11], 71), 0),
        "decay_rates": jnp.clip(jnp.exp(jax.random.uniform(key_list[5], (SHARED_HEADS,), jnp.float32, math.log(0.7), math.log(1.4))), 0.7, 1.4),
        "skip_gains": jnp.clip(jax.random.uniform(key_list[6], (SHARED_HEADS,), jnp.float32, 0.5, 1.5), 0.5, 1.5),
        "pre_gain": jnp.clip(1.0 + 0.15 * jax.random.normal(key_list[7], (HD,), jnp.float32), 0.25, 1.75),
        "state_in_weight": normal_values(key_list[8], (HD, STATE), HD ** -0.5, 0.125),
        "state_out_weight": normal_values(key_list[9], (HD, STATE), HD ** -0.5, 0.125),
        "post_gain": jnp.clip(1.0 + 0.15 * jax.random.normal(key_list[10], (HD,), jnp.float32), 0.25, 1.75),
    }


def rms_scale(values, gain_row):
    return values * lax.rsqrt(lax.optimization_barrier(jnp.mean(values * values, axis=-1, keepdims=True)) + 1e-05) * gain_row

def attend_frame(frame_arrays, block_lists):
    query_frame, key_frame, value_frame = frame_arrays
    block_count = FTOK // BLOCK
    group_size = math.gcd(block_count, max(1, 512 // BLOCK))
    list_width = block_lists.shape[1]
    score_scale = 1.0 / math.sqrt(HEAD_DIM)
    query_blocks = query_frame.reshape(block_count, BLOCK, SHARED_HEADS, HEAD_DIM)
    key_blocks = key_frame.reshape(block_count, BLOCK, SHARED_HEADS, HEAD_DIM)
    value_blocks = value_frame.reshape(block_count, BLOCK, SHARED_HEADS, HEAD_DIM)

    def attend_group(group_index):
        first_block = (group_index * group_size).astype(jnp.int32)
        chosen = lax.dynamic_slice_in_dim(block_lists, first_block, group_size, 0)
        query_group = lax.dynamic_slice_in_dim(query_blocks, first_block, group_size, 0).astype(jnp.float32)
        key_group = jnp.take(key_blocks, chosen, axis=0).reshape(group_size, list_width * BLOCK, SHARED_HEADS, HEAD_DIM).astype(jnp.float32)
        value_group = jnp.take(value_blocks, chosen, axis=0).reshape(group_size, list_width * BLOCK, SHARED_HEADS, HEAD_DIM).astype(jnp.float32)
        scores = jnp.einsum('gqhd,gkhd->ghqk', query_group, key_group) * score_scale
        row_max = lax.optimization_barrier(jnp.max(scores, axis=-1, keepdims=True))
        exp_scores = jnp.exp(scores - row_max)
        totals = lax.optimization_barrier(jnp.sum(exp_scores, axis=-1))
        weights_bf = lax.optimization_barrier(exp_scores.astype(jnp.bfloat16)).astype(jnp.float32)
        summed = jnp.einsum('ghqk,gkhd->gqhd', weights_bf, value_group)
        return (summed / jnp.transpose(totals, (0, 2, 1))[..., None]).astype(jnp.bfloat16)
    attended = lax.map(attend_group, jnp.arange(block_count // group_size, dtype=jnp.int32))
    return attended.reshape(FTOK, SHARED_HEADS * HEAD_DIM)

def temporal_mix(normed, step_block, decay_rates, skip_gains, state_in_weight, state_out_weight, post_gain):
    frame_count, token_count, channel_count = normed.shape
    head_count = step_block.shape[2]
    head_width = channel_count // head_count
    flat_rows = normed.reshape(frame_count * token_count, channel_count)
    b_in = jnp.dot(flat_rows, state_in_weight, preferred_element_type=jnp.float32).reshape(frame_count, token_count, -1)
    c_out = jnp.dot(flat_rows, state_out_weight, preferred_element_type=jnp.float32).reshape(frame_count, token_count, -1)
    gram_matrix = jnp.einsum('tkn,skn->kts', c_out, b_in, precision=lax.Precision.HIGHEST)
    log_decay = -step_block * decay_rates
    frame_index = jnp.arange(frame_count, dtype=jnp.int32)
    between = ((frame_index[None, :, None] < frame_index[None, None, :]) & (frame_index[None, None, :] <= frame_index[:, None, None])).astype(jnp.float32)
    seg_sum = jnp.einsum('tsr,rkh->ktsh', between, log_decay, precision=lax.Precision.HIGHEST)
    causal = frame_index[None, :] <= frame_index[:, None]
    decay_matrix = jnp.where(causal[None, :, :, None], jnp.exp(seg_sum), jnp.zeros_like(seg_sum))
    weight_matrix = gram_matrix[..., None] * decay_matrix * jnp.transpose(step_block, (1, 0, 2))[:, None, :, :]
    x_values = normed.astype(jnp.float32).reshape(frame_count, token_count, head_count, head_width)
    y_mixed = jnp.einsum('ktsh,skhp->tkhp', weight_matrix, x_values, precision=lax.Precision.HIGHEST) + skip_gains[:, None] * x_values
    y_flat = y_mixed.reshape(frame_count, token_count, channel_count)
    return rms_scale(y_flat, post_gain).astype(jnp.bfloat16)

def reference(queries, key_vectors, value_vectors, block_lists, step_sizes, decay_rates, skip_gains, pre_gain, state_in_weight, state_out_weight, post_gain):
    attended = lax.map(partial(attend_frame, block_lists=block_lists), (queries, key_vectors, value_vectors))
    normed = rms_scale(attended.astype(jnp.float32), pre_gain).astype(jnp.bfloat16)

    def mix_block(block_index):
        start_row = (block_index * BLOCK).astype(jnp.int32)
        normed_block = lax.dynamic_slice_in_dim(normed, start_row, BLOCK, 1)
        step_block = lax.dynamic_slice_in_dim(step_sizes, start_row, BLOCK, 1)
        return temporal_mix(normed_block, step_block, decay_rates, skip_gains, state_in_weight, state_out_weight, post_gain)
    mixed_blocks = lax.map(mix_block, jnp.arange(FTOK // BLOCK, dtype=jnp.int32))
    return jnp.transpose(mixed_blocks, (1, 0, 2, 3)).reshape(LATENT_FRAMES, FTOK, SHARED_HEADS * HEAD_DIM)
```

```python
import functools
import math

import jax
import jax.numpy as jnp
from jax import lax
from jax.experimental import pallas as pl
from jax.experimental.pallas import tpu as pltpu
from jax.sharding import PartitionSpec as P

SHARED_HEADS = 16
HEAD_DIM = 128
ROWS = 8
PER_CHUNK = 2
AHEAD = 2
LAG_MERGE = 1
LAG_MIX = 3
KV_PARTS = 2
EXTRA = 128
VMEM_BYTES = 63 * 1024 * 1024
MESH = pl.DeviceIdType.MESH
F32 = jnp.float32
BF16 = jnp.bfloat16
HIGH = lax.Precision.HIGHEST


def remote(src, dst, send_sem, recv_sem, axis, index):
    return pltpu.make_async_remote_copy(
        src_ref=src,
        dst_ref=dst,
        send_sem=send_sem,
        recv_sem=recv_sem,
        device_id={axis: index},
        device_id_type=MESH,
    )


def loop(low, high, act):
    if high - low == 1:
        act(low)
    elif high > low:

        def turn(i, carry):
            act(i)
            return carry

        lax.fori_loop(low, high, turn, 0)


def lanes_of(head):
    return slice(head * HEAD_DIM, (head + 1) * HEAD_DIM)


def attend(query, key, value, bias, heads):
    factor = math.log2(math.e) / math.sqrt(HEAD_DIM)
    across = (((1,), (1,)), ((), ()))
    scores = [
        lax.dot_general(query(h), key(h), across, preferred_element_type=F32) * factor + bias
        for h in heads
    ]
    tops = [jnp.max(s, axis=-1, keepdims=True) for s in scores]
    weights = [jnp.exp2(s - m) for s, m in zip(scores, tops)]
    totals = [jnp.sum(w, axis=-1, keepdims=True) for w in weights]
    sums = [
        jnp.dot(w.astype(BF16), value(h), preferred_element_type=F32) for w, h in zip(weights, heads)
    ]
    return [s / t for s, t in zip(sums, totals)], tops, totals


def packed(columns, heads, lane, into):
    for h, column in zip(heads, columns):
        into = jnp.where(lane == h, column, into)
    return into


def kernel(
    dims,
    lists_hbm,
    rates_hbm,
    skips_hbm,
    q_hbm,
    k_hbm,
    v_hbm,
    steps_hbm,
    pre_hbm,
    w_in_hbm,
    w_out_hbm,
    post_hbm,
    out_ref,
    lists_ref,
    rates_ref,
    skips_ref,
    q_ref,
    steps_ref,
    pre_ref,
    w_in_ref,
    w_out_ref,
    post_ref,
    kv_buf,
    qr_buf,
    ps_buf,
    pr_buf,
    ol_buf,
    ll_buf,
    n_buf,
    x_buf,
    o_buf,
    d_buf,
    load_sem,
    own_sem,
    kv_send,
    kv_recv,
    step_send,
    step_recv,
    step_own,
    q_send,
    q_recv,
    p_send,
    p_recv,
    a_send,
    a_recv,
    l_send,
    l_recv,
    o_send,
    o_recv,
    self_sem,
    home_sem,
):
    space_count, tm_count, list_width = dims
    half_count, turns, _, channels = q_hbm.shape
    tokens = half_count * turns * ROWS
    per_chunk = PER_CHUNK
    sets = half_count // per_chunk
    chunks = sets * turns
    rows = per_chunk * ROWS
    chips = space_count // 2
    all_heads = range(SHARED_HEADS)
    space = lax.axis_index("space")
    tm = lax.axis_index("tm")
    half = tm // half_count
    place = tm % half_count
    chip = space // 2
    core = space % 2
    partner = chip * 2 + 1 - core

    barrier = pltpu.get_barrier_semaphore()

    def greet_chip(step):
        peer = lax.rem(chip + step, chips) * 2 + core
        pl.semaphore_signal(barrier, inc=1, device_id={"space": peer}, device_id_type=MESH)

    def greet_frame(step):
        peer = lax.rem(tm + step, tm_count)
        pl.semaphore_signal(barrier, inc=1, device_id={"tm": peer}, device_id_type=MESH)

    pl.semaphore_signal(barrier, inc=1, device_id={"space": partner}, device_id_type=MESH)
    loop(1, chips, greet_chip)
    loop(1, tm_count, greet_frame)

    part_width = channels // KV_PARTS

    def kv_span(part):
        return pl.ds(part * part_width, part_width)

    def own_kv(which, part):
        source = (k_hbm, v_hbm)[which]
        return pltpu.make_async_copy(
            source.at[:, kv_span(part)],
            kv_buf.at[which, core, :, kv_span(part)],
            own_sem.at[which, part],
        )

    def partner_kv(which, part):
        source = (k_hbm, v_hbm)[which]
        return remote(
            source.at[:, kv_span(part)],
            kv_buf.at[which, core, :, kv_span(part)],
            kv_send.at[which, part],
            kv_recv.at[which, part],
            "space",
            partner,
        )

    load_q = pltpu.make_async_copy(q_hbm, q_ref, load_sem.at[0])
    load_q.start()
    for part in range(KV_PARTS):
        for which in range(2):
            own_kv(which, part).start()
    loads = [
        pltpu.make_async_copy(source, target, load_sem.at[1 + index])
        for index, (source, target) in enumerate(
            (
                (lists_hbm, lists_ref),
                (rates_hbm, rates_ref),
                (skips_hbm, skips_ref),
                (pre_hbm, pre_ref),
                (w_in_hbm, w_in_ref),
                (w_out_hbm, w_out_ref),
                (post_hbm, post_ref),
            )
        )
    ]
    for load in loads:
        load.start()

    def chunk_groups(c):
        return c // sets, (sets - 1 - c % sets) * per_chunk

    def query_out(c, step):
        turn, first = chunk_groups(c)
        return remote(
            q_hbm.at[pl.ds(first, per_chunk), turn],
            qr_buf.at[step - 1, c],
            q_send.at[step - 1, c],
            q_recv.at[step - 1, c],
            "space",
            lax.rem(chip + step, chips) * 2 + core,
        )

    def partial_out(c, step):
        return remote(
            ps_buf.at[step - 1, c],
            pr_buf.at[step - 1, c],
            p_send.at[step - 1, c],
            p_recv.at[step - 1, c],
            "space",
            lax.rem(chip - step + chips, chips) * 2 + core,
        )

    def send_query(c):
        loop(1, chips, lambda step: query_out(c, step).start())

    pl.semaphore_wait(barrier, chips + tm_count - 1)

    send_query(0)
    for part in range(KV_PARTS):
        for which in range(2):
            partner_kv(which, part).start()
    for c in range(1, min(AHEAD, chunks)):
        send_query(c)

    def step_copy(which, target, part):
        return remote(
            steps_hbm,
            steps_ref.at[:, part],
            step_send.at[which],
            step_recv.at[part],
            "tm",
            target,
        )

    def step_local(part):
        return pltpu.make_async_copy(steps_hbm, steps_ref.at[:, part], step_own.at[part])

    for which in range(2):
        target = which * half_count + tm // 2
        part = tm % 2

        @pl.when(target != tm)
        def _():
            step_copy(which, target, part).start()

        @pl.when(target == tm)
        def _():
            step_local(part).start()

    for load in loads:
        load.wait()
    load_q.wait()

    def key_of(h):
        return kv_buf[0, :, :, lanes_of(h)].reshape(2 * tokens, HEAD_DIM)

    def value_of(h):
        return kv_buf[1, :, :, lanes_of(h)].reshape(2 * tokens, HEAD_DIM)

    block_of = chip * 2 + lax.broadcasted_iota(jnp.int32, (1, 2 * tokens), 1) // tokens

    def bias_of(owner):
        chosen = block_of == lists_ref[owner, 0]
        for entry in range(1, list_width):
            chosen = chosen | (block_of == lists_ref[owner, entry])
        return jnp.where(chosen, 0.0, -1e30).astype(F32)

    lane_of = lax.broadcasted_iota(jnp.int32, (tokens, HEAD_DIM), 1)
    slot_of = lane_of % SHARED_HEADS
    tops = jnp.zeros((tokens, HEAD_DIM), F32)
    totals = jnp.ones((tokens, HEAD_DIM), F32)
    bias = bias_of(space)
    heads_part = SHARED_HEADS // KV_PARTS
    for part in range(KV_PARTS):
        for which in range(2):
            own_kv(which, part).wait()
            partner_kv(which, part).wait_recv()
        for first in range(part * heads_part, (part + 1) * heads_part, 4):
            heads = range(first, first + 4)
            summed, top, total = attend(
                lambda h: q_ref[:, :, :, lanes_of(h)].reshape(tokens, HEAD_DIM),
                key_of,
                value_of,
                bias,
                heads,
            )
            for h, values in zip(heads, summed):
                ol_buf[:, :, :, lanes_of(h)] = values.reshape(half_count, turns, ROWS, HEAD_DIM)
            tops = packed(top, heads, slot_of, tops)
            totals = packed(total, heads, slot_of, totals)
    ll_buf[...] = (tops + jnp.log2(totals)).reshape(half_count, turns, ROWS, HEAD_DIM)

    own_rows = half_count * ROWS
    both_rows = tm_count * ROWS

    def make_decays():
        for part in range(2):
            origin = 2 * place + part

            @pl.when(origin != tm)
            def _():
                step_copy(0, origin, part).wait_recv()

            @pl.when(origin == tm)
            def _():
                step_local(part).wait()

        steps = steps_ref[...].reshape(tm_count, turns, ROWS, SHARED_HEADS)
        earlier, later = steps[:half_count], steps[half_count:]
        own = jnp.where(half == 1, later, earlier)
        steps = jnp.concatenate([earlier, own], axis=0)
        counted = jnp.concatenate([jnp.where(half == 1, earlier, 0.0), own], axis=0)
        run = [counted[0]]
        for frame in range(1, tm_count):
            run.append(run[-1] + counted[frame])
        run = jnp.stack(run)
        row = half_count * ROWS + lax.broadcasted_iota(jnp.int32, (own_rows, both_rows), 0)
        col = lax.broadcasted_iota(jnp.int32, (own_rows, both_rows), 1)
        counts = (row % ROWS == col % ROWS) & (col // ROWS <= row // ROWS)
        counts = counts & (col >= (1 - half) * own_rows)
        for turn in range(turns):
            total = run[:, turn].reshape(both_rows, SHARED_HEADS)
            total_t = jnp.transpose(total)
            steps_t = jnp.transpose(steps[:, turn].reshape(both_rows, SHARED_HEADS))
            for head in all_heads:
                gap = total_t[head : head + 1, :] - total[own_rows:, head : head + 1]
                decay = jnp.exp(jnp.where(counts, gap * rates_ref[head], -1e30))
                d_buf[turn, head] = decay * steps_t[head : head + 1, :]

    make_decays()

    @pl.when(half == 0)
    def _():
        x_buf[:, 0:half_count] = jnp.zeros((turns, half_count, ROWS, channels), BF16)

    chunk_lane = lax.broadcasted_iota(jnp.int32, (rows, HEAD_DIM), 1)
    chunk_slot = chunk_lane % SHARED_HEADS

    def attend_for(c, step):
        query_out(c, step).wait_recv()
        owner = lax.rem(chip - step + chips, chips) * 2 + core
        query = qr_buf[step - 1, c].reshape(rows, channels)
        summed, top, total = attend(
            lambda h: query[:, lanes_of(h)], key_of, value_of, bias_of(owner), all_heads
        )
        for h, values in zip(all_heads, summed):
            ps_buf[step - 1, c, :, lanes_of(h)] = values.astype(BF16)
        tops = packed(top, all_heads, chunk_slot, jnp.zeros((rows, HEAD_DIM), F32))
        totals = packed(total, all_heads, chunk_slot, jnp.ones((rows, HEAD_DIM), F32))
        logs = tops + jnp.log2(totals)
        big = logs.astype(BF16)
        rest = logs - big.astype(F32)
        middle = rest.astype(BF16)
        small = (rest - middle.astype(F32)).astype(BF16)
        extra = jnp.where(
            chunk_lane < SHARED_HEADS,
            big.astype(F32),
            jnp.where(chunk_lane < 2 * SHARED_HEADS, middle.astype(F32), small.astype(F32)),
        )
        ps_buf[step - 1, c, :, channels : channels + EXTRA] = extra.astype(BF16)
        partial_out(c, step).start()

    def rows_out(group, turn, peer):
        return remote(
            n_buf.at[turn, group],
            x_buf.at[turn, half_count + place],
            a_send.at[turn, group],
            a_recv.at[turn, place],
            "tm",
            half * half_count + peer,
        )

    def rows_later(group, turn, peer):
        return remote(
            n_buf.at[turn, group],
            x_buf.at[turn, place],
            l_send.at[turn, group],
            l_recv.at[turn, place],
            "tm",
            half_count + peer,
        )

    def rows_in(turn, sender):
        return remote(
            n_buf.at[turn, 0],
            x_buf.at[turn, half_count + sender],
            a_send.at[turn, 0],
            a_recv.at[turn, sender],
            "tm",
            half * half_count + sender,
        )

    def earlier_in(turn, sender):
        return remote(
            n_buf.at[turn, 0],
            x_buf.at[turn, sender],
            l_send.at[turn, 0],
            l_recv.at[turn, sender],
            "tm",
            sender,
        )

    def rows_home(turn):
        return pltpu.make_async_copy(
            n_buf.at[turn, place], x_buf.at[turn, half_count + place], self_sem.at[turn]
        )

    def merge(c):
        turn, first = chunk_groups(c)
        loop(1, chips, lambda step: partial_out(c, step).wait_recv())
        logs = [ll_buf[pl.ds(first, per_chunk), turn].reshape(rows, HEAD_DIM)]
        for step in range(1, chips):
            extra = pr_buf[step - 1, c, :, channels : channels + EXTRA].astype(F32)
            once = pltpu.roll(extra, EXTRA - SHARED_HEADS, 1)
            twice = pltpu.roll(extra, EXTRA - 2 * SHARED_HEADS, 1)
            logs.append(extra + (once + twice))
        top = functools.reduce(jnp.maximum, logs)
        shares = [jnp.exp2(log - top) for log in logs]
        total = functools.reduce(jnp.add, shares)
        shares = [share / total for share in shares]
        attended = []
        for h in all_heads:
            value = shares[0][:, h : h + 1] * ol_buf[
                pl.ds(first, per_chunk), turn, :, lanes_of(h)
            ].reshape(rows, HEAD_DIM)
            for step in range(1, chips):
                value = value + shares[step][:, h : h + 1] * pr_buf[
                    step - 1, c, :, lanes_of(h)
                ].astype(F32)
            attended.append(value.astype(BF16).astype(F32))
        squares = functools.reduce(jnp.add, [a * a for a in attended])
        mean = jnp.sum(squares, axis=-1, keepdims=True) / channels
        scale = lax.rsqrt(mean + 1e-05)
        for h in all_heads:
            normed = attended[h] * scale * pre_ref[:, lanes_of(h)]
            n_buf[turn, pl.ds(first, per_chunk), :, lanes_of(h)] = normed.reshape(
                per_chunk, ROWS, HEAD_DIM
            ).astype(BF16)
        for index in range(per_chunk):
            peer = first + index

            @pl.when(half == 0)
            def _():
                rows_later(peer, turn, peer).start()

            @pl.when(peer != place)
            def _():
                rows_out(peer, turn, peer).start()

            @pl.when(peer == place)
            def _():
                rows_home(turn).start()

    def result_out(turn, step):
        peer = lax.rem(place + step, half_count)
        return remote(
            o_buf.at[turn, peer],
            out_ref.at[place, turn],
            o_send.at[turn, step],
            o_recv.at[turn, step],
            "tm",
            half * half_count + peer,
        )

    def result_in(turn, step):
        sender = lax.rem(place - step + half_count, half_count)
        return remote(
            o_buf.at[turn, sender],
            out_ref.at[sender, turn],
            o_send.at[turn, step],
            o_recv.at[turn, step],
            "tm",
            half * half_count + sender,
        )

    def result_home(turn):
        return pltpu.make_async_copy(
            o_buf.at[turn, place], out_ref.at[place, turn], home_sem.at[turn]
        )

    def mix(turn):
        def take(step):
            rows_in(turn, lax.rem(place - step + half_count, half_count)).wait_recv()

        loop(1, half_count, take)
        rows_home(turn).wait()

        @pl.when(half == 1)
        def _():
            loop(0, half_count, lambda sender: earlier_in(turn, sender).wait_recv())

        values = x_buf[turn].reshape(both_rows, channels)
        across = (((1,), (1,)), ((), ()))
        b_in = lax.dot_general(values, w_in_ref[...], across, preferred_element_type=F32)
        c_out = lax.dot_general(
            values[own_rows:], w_out_ref[...], across, preferred_element_type=F32
        )
        gram = lax.dot_general(c_out, b_in, across, precision=HIGH, preferred_element_type=F32)
        mixing = [(gram * d_buf[turn, h]).astype(BF16) for h in all_heads]
        mixed = [
            jnp.dot(m, values[:, lanes_of(h)], preferred_element_type=F32)
            for m, h in zip(mixing, all_heads)
        ]
        mixed = [
            m + skips_ref[h] * values[own_rows:, lanes_of(h)].astype(F32)
            for m, h in zip(mixed, all_heads)
        ]
        squares = functools.reduce(jnp.add, [m * m for m in mixed])
        mean = jnp.sum(squares, axis=-1, keepdims=True) / channels
        scale = lax.rsqrt(mean + 1e-05)
        for h in all_heads:
            result = mixed[h] * scale * post_ref[:, lanes_of(h)]
            o_buf[turn, :, :, lanes_of(h)] = result.reshape(half_count, ROWS, HEAD_DIM).astype(BF16)
        loop(1, half_count, lambda step: result_out(turn, step).start())
        result_home(turn).start()

    def turn_of_loop(i):
        @pl.when(i + AHEAD < chunks)
        def _():
            send_query(i + AHEAD)

        @pl.when(i < chunks)
        def _():
            loop(1, chips, lambda step: attend_for(i, step))

        @pl.when((i >= LAG_MERGE) & (i < chunks + LAG_MERGE))
        def _():
            merge(i - LAG_MERGE)

        c = i - LAG_MIX
        turn, first = chunk_groups(jnp.maximum(c, 0))

        @pl.when((c >= 0) & (place >= first) & (place < first + per_chunk))
        def _():
            mix(turn)

    loop(0, chunks + LAG_MIX, turn_of_loop)

    for part in range(KV_PARTS):
        for which in range(2):
            partner_kv(which, part).wait_send()
    for which in range(2):
        target = which * half_count + tm // 2

        @pl.when(target != tm)
        def _():
            step_copy(which, target, tm % 2).wait_send()

    def sent_chunk(c):
        def sent(step):
            query_out(c, step).wait_send()
            partial_out(c, step).wait_send()

        loop(1, chips, sent)

    loop(0, chunks, sent_chunk)

    for turn in range(turns):

        def sent_rows(group):
            @pl.when(half == 0)
            def _():
                rows_later(group, turn, group).wait_send()

            @pl.when(group != place)
            def _():
                rows_out(group, turn, group).wait_send()

        loop(0, half_count, sent_rows)

    for turn in range(turns):

        def finish(step):
            result_out(turn, step).wait_send()
            result_in(turn, step).wait_recv()

        loop(1, half_count, finish)
        result_home(turn).wait()


def body(
    queries,
    key_vectors,
    value_vectors,
    block_lists,
    step_sizes,
    decay_rates,
    skip_gains,
    pre_gain,
    state_in_weight,
    state_out_weight,
    post_gain,
):
    tokens, channels = queries.shape[1], queries.shape[2]
    space_count = lax.axis_size("space")
    tm_count = lax.axis_size("tm")
    half_count = tm_count // 2
    turns = tokens // (half_count * ROWS)
    chips = space_count // 2
    chunks = half_count * turns // PER_CHUNK
    rows = PER_CHUNK * ROWS
    state = state_in_weight.shape[1]
    hbm = pl.BlockSpec(memory_space=pl.ANY)
    dma = pltpu.SemaphoreType.DMA
    out = pl.pallas_call(
        functools.partial(kernel, (space_count, tm_count, block_lists.shape[1])),
        out_shape=jax.ShapeDtypeStruct((half_count, turns, ROWS, channels), BF16),
        in_specs=[hbm] * 11,
        out_specs=hbm,
        scratch_shapes=[
            pltpu.SMEM(block_lists.shape, jnp.int32),
            pltpu.SMEM(decay_rates.shape, F32),
            pltpu.SMEM(skip_gains.shape, F32),
            pltpu.VMEM((half_count, turns, ROWS, channels), BF16),
            pltpu.VMEM((tm_count, 2, tokens // tm_count, SHARED_HEADS), F32),
            pltpu.VMEM((1, channels), F32),
            pltpu.VMEM((state, channels), BF16),
            pltpu.VMEM((state, channels), BF16),
            pltpu.VMEM((1, channels), F32),
            pltpu.VMEM((2, 2, tokens, channels), BF16),
            pltpu.VMEM((chips - 1, chunks, PER_CHUNK, ROWS, channels), BF16),
            pltpu.VMEM((chips - 1, chunks, rows, channels + EXTRA), BF16),
            pltpu.VMEM((chips - 1, chunks, rows, channels + EXTRA), BF16),
            pltpu.VMEM((half_count, turns, ROWS, channels), F32),
            pltpu.VMEM((half_count, turns, ROWS, HEAD_DIM), F32),
            pltpu.VMEM((turns, half_count, ROWS, channels), BF16),
            pltpu.VMEM((turns, tm_count, ROWS, channels), BF16),
            pltpu.VMEM((turns, half_count, ROWS, channels), BF16),
            pltpu.VMEM((turns, SHARED_HEADS, half_count * ROWS, tm_count * ROWS), F32),
            dma((8,)),
            dma((2, KV_PARTS)),
            dma((2, KV_PARTS)),
            dma((2, KV_PARTS)),
            dma((2,)),
            dma((2,)),
            dma((2,)),
            dma((chips - 1, chunks)),
            dma((chips - 1, chunks)),
            dma((chips - 1, chunks)),
            dma((chips - 1, chunks)),
            dma((turns, half_count)),
            dma((turns, half_count)),
            dma((turns, half_count)),
            dma((turns, half_count)),
            dma((turns, half_count)),
            dma((turns, half_count)),
            dma((turns,)),
            dma((turns,)),
        ],
        compiler_params=pltpu.CompilerParams(
            collective_id=0, has_side_effects=True, vmem_limit_bytes=VMEM_BYTES
        ),
        name="attend_and_mix",
    )(
        block_lists,
        decay_rates,
        skip_gains,
        queries.reshape(half_count, turns, ROWS, channels),
        key_vectors.reshape(tokens, channels),
        value_vectors.reshape(tokens, channels),
        step_sizes,
        pre_gain.reshape(1, channels),
        state_in_weight.T,
        state_out_weight.T,
        post_gain.reshape(1, channels),
    )
    return out.reshape(1, tokens, channels)


def solution(mesh):
    placed = (
        P("tm", "space", None),
        P("tm", "space", None),
        P("tm", "space", None),
        P(),
        P(None, ("space", "tm"), None),
        P(),
        P(),
        P(),
        P(),
        P(),
        P(),
    )
    return jax.shard_map(
        body, mesh=mesh, in_specs=placed, out_specs=P("tm", "space", None), check_vma=False
    )
```

```python
import functools
import math

import jax
import jax.numpy as jnp
from jax import lax
from jax.experimental import pallas as pl
from jax.experimental.pallas import tpu as pltpu
from jax.sharding import PartitionSpec as P

SHARED_HEADS = 16
HEAD_DIM = 128
ROWS = 8
PER_CHUNK = 1
AHEAD = 4
LAG_MERGE = 3
LAG_MIX = 7
KV_PARTS = 2
EXTRA = 128
VMEM_BYTES = 44 * 1024 * 1024
MESH = pl.DeviceIdType.MESH
F32 = jnp.float32
BF16 = jnp.bfloat16
HIGH = lax.Precision.HIGHEST


def remote(src, dst, send_sem, recv_sem, axis, index):
    return pltpu.make_async_remote_copy(
        src_ref=src,
        dst_ref=dst,
        send_sem=send_sem,
        recv_sem=recv_sem,
        device_id={axis: index},
        device_id_type=MESH,
    )


def loop(low, high, act):
    if high - low == 1:
        act(low)
    elif high > low:

        def turn(i, carry):
            act(i)
            return carry

        lax.fori_loop(low, high, turn, 0)


def lanes_of(head):
    return slice(head * HEAD_DIM, (head + 1) * HEAD_DIM)


def attend(query, key, value, bias, heads):
    factor = math.log2(math.e) / math.sqrt(HEAD_DIM)
    across = (((1,), (1,)), ((), ()))
    scores = [
        lax.dot_general(query(h), key(h), across, preferred_element_type=F32) * factor + bias
        for h in heads
    ]
    tops = [jnp.max(s, axis=-1, keepdims=True) for s in scores]
    weights = [jnp.exp2(s - m) for s, m in zip(scores, tops)]
    totals = [jnp.sum(w, axis=-1, keepdims=True) for w in weights]
    sums = [
        jnp.dot(w.astype(BF16), value(h), preferred_element_type=F32) for w, h in zip(weights, heads)
    ]
    return [s / t for s, t in zip(sums, totals)], tops, totals


def packed(columns, heads, lane, into):
    for h, column in zip(heads, columns):
        into = jnp.where(lane == h, column, into)
    return into


def kernel(
    dims,
    lists_hbm,
    rates_hbm,
    skips_hbm,
    q_hbm,
    k_hbm,
    v_hbm,
    steps_hbm,
    pre_hbm,
    w_in_hbm,
    w_out_hbm,
    post_hbm,
    out_ref,
    lists_ref,
    rates_ref,
    skips_ref,
    q_ref,
    steps_ref,
    pre_ref,
    w_in_ref,
    w_out_ref,
    post_ref,
    kv_buf,
    qr_buf,
    ps_buf,
    pr_buf,
    ol_buf,
    ll_buf,
    n_buf,
    x_buf,
    o_buf,
    d_buf,
    load_sem,
    own_sem,
    kv_send,
    kv_recv,
    step_send,
    step_recv,
    step_own,
    q_send,
    q_recv,
    p_send,
    p_recv,
    a_send,
    a_recv,
    l_send,
    l_recv,
    o_send,
    o_recv,
    self_sem,
    home_sem,
    ready_sem,
):
    space_count, tm_count, list_width = dims
    half_count, turns, _, channels = q_hbm.shape
    tokens = half_count * turns * ROWS
    per_chunk = PER_CHUNK
    sets = half_count // per_chunk
    chunks = sets * turns
    rows = per_chunk * ROWS
    chips = space_count // 2
    all_heads = range(SHARED_HEADS)
    space = lax.axis_index("space")
    tm = lax.axis_index("tm")
    half = tm // half_count
    place = tm % half_count
    chip = space // 2
    core = space % 2
    partner = chip * 2 + 1 - core

    barrier = pltpu.get_barrier_semaphore()

    def greet_chip(step):
        peer = lax.rem(chip + step, chips) * 2 + core
        pl.semaphore_signal(barrier, inc=1, device_id={"space": peer}, device_id_type=MESH)

    def greet_frame(peer):
        pl.semaphore_signal(barrier, inc=1, device_id={"tm": peer}, device_id_type=MESH)

    def answer_frame(peer):
        pl.semaphore_signal(ready_sem, inc=1, device_id={"tm": peer}, device_id_type=MESH)

    pl.semaphore_signal(barrier, inc=1, device_id={"space": partner}, device_id_type=MESH)
    loop(1, chips, greet_chip)
    lax.fori_loop(tm + 1, tm_count, lambda peer, carry: (greet_frame(peer), carry)[1], 0)

    part_width = channels // KV_PARTS

    def kv_span(part):
        return pl.ds(part * part_width, part_width)

    def own_kv(which, part):
        source = (k_hbm, v_hbm)[which]
        return pltpu.make_async_copy(
            source.at[:, kv_span(part)],
            kv_buf.at[which, core, :, kv_span(part)],
            own_sem.at[which, part],
        )

    def partner_kv(which, part):
        source = (k_hbm, v_hbm)[which]
        return remote(
            source.at[:, kv_span(part)],
            kv_buf.at[which, core, :, kv_span(part)],
            kv_send.at[which, part],
            kv_recv.at[which, part],
            "space",
            partner,
        )

    load_q = pltpu.make_async_copy(q_hbm, q_ref, load_sem.at[0])
    load_q.start()
    for part in range(KV_PARTS):
        for which in range(2):
            own_kv(which, part).start()
    loads = [
        pltpu.make_async_copy(source, target, load_sem.at[1 + index])
        for index, (source, target) in enumerate(
            (
                (lists_hbm, lists_ref),
                (rates_hbm, rates_ref),
                (skips_hbm, skips_ref),
                (pre_hbm, pre_ref),
                (w_in_hbm, w_in_ref),
                (w_out_hbm, w_out_ref),
                (post_hbm, post_ref),
            )
        )
    ]
    for load in loads:
        load.start()

    def chunk_groups(c):
        return c // sets, (sets - 1 - c % sets) * per_chunk

    def query_out(c, step):
        turn, first = chunk_groups(c)
        return remote(
            q_hbm.at[pl.ds(first, per_chunk), turn],
            qr_buf.at[step - 1, c],
            q_send.at[step - 1, c],
            q_recv.at[step - 1, c],
            "space",
            lax.rem(chip + step, chips) * 2 + core,
        )

    def partial_out(c, step):
        return remote(
            ps_buf.at[step - 1, c],
            pr_buf.at[step - 1, c],
            p_send.at[step - 1, c],
            p_recv.at[step - 1, c],
            "space",
            lax.rem(chip - step + chips, chips) * 2 + core,
        )

    def send_query(c):
        loop(1, chips, lambda step: query_out(c, step).start())

    pl.semaphore_wait(barrier, chips + tm)

    send_query(0)
    for part in range(KV_PARTS):
        for which in range(2):
            partner_kv(which, part).start()
    for c in range(1, min(AHEAD, chunks)):
        send_query(c)
    lax.fori_loop(0, tm, lambda peer, carry: (answer_frame(peer), carry)[1], 0)

    def step_copy(which, target, part):
        return remote(
            steps_hbm,
            steps_ref.at[:, part],
            step_send.at[which],
            step_recv.at[part],
            "tm",
            target,
        )

    def step_local(part):
        return pltpu.make_async_copy(steps_hbm, steps_ref.at[:, part], step_own.at[part])

    for load in loads:
        load.wait()
    load_q.wait()

    def key_of(h):
        return kv_buf[0, :, :, lanes_of(h)].reshape(2 * tokens, HEAD_DIM)

    def value_of(h):
        return kv_buf[1, :, :, lanes_of(h)].reshape(2 * tokens, HEAD_DIM)

    block_of = chip * 2 + lax.broadcasted_iota(jnp.int32, (1, 2 * tokens), 1) // tokens

    def bias_of(owner):
        chosen = block_of == lists_ref[owner, 0]
        for entry in range(1, list_width):
            chosen = chosen | (block_of == lists_ref[owner, entry])
        return jnp.where(chosen, 0.0, -1e30).astype(F32)

    lane_of = lax.broadcasted_iota(jnp.int32, (tokens, HEAD_DIM), 1)
    slot_of = lane_of % SHARED_HEADS
    tops = jnp.zeros((tokens, HEAD_DIM), F32)
    totals = jnp.ones((tokens, HEAD_DIM), F32)
    bias = bias_of(space)
    heads_part = SHARED_HEADS // KV_PARTS
    for part in range(KV_PARTS):
        for which in range(2):
            own_kv(which, part).wait()
            partner_kv(which, part).wait_recv()
        for first in range(part * heads_part, (part + 1) * heads_part, 4):
            heads = range(first, first + 4)
            summed, top, total = attend(
                lambda h: q_ref[:, :, :, lanes_of(h)].reshape(tokens, HEAD_DIM),
                key_of,
                value_of,
                bias,
                heads,
            )
            for h, values in zip(heads, summed):
                ol_buf[:, :, :, lanes_of(h)] = values.reshape(half_count, turns, ROWS, HEAD_DIM)
            tops = packed(top, heads, slot_of, tops)
            totals = packed(total, heads, slot_of, totals)
    ll_buf[...] = (tops + jnp.log2(totals)).reshape(half_count, turns, ROWS, HEAD_DIM)

    @pl.when(tm < tm_count - 1)
    def _():
        pl.semaphore_wait(ready_sem, tm_count - 1 - tm)

    for which in range(2):
        target = which * half_count + tm // 2
        part = tm % 2

        @pl.when(target != tm)
        def _():
            step_copy(which, target, part).start()

        @pl.when(target == tm)
        def _():
            step_local(part).start()

    own_rows = half_count * ROWS
    both_rows = tm_count * ROWS

    def make_decays():
        for part in range(2):
            origin = 2 * place + part

            @pl.when(origin != tm)
            def _():
                step_copy(0, origin, part).wait_recv()

            @pl.when(origin == tm)
            def _():
                step_local(part).wait()

        steps = steps_ref[...].reshape(tm_count, turns, ROWS, SHARED_HEADS)
        earlier, later = steps[:half_count], steps[half_count:]
        own = jnp.where(half == 1, later, earlier)
        steps = jnp.concatenate([earlier, own], axis=0)
        counted = jnp.concatenate([jnp.where(half == 1, earlier, 0.0), own], axis=0)
        run = [counted[0]]
        for frame in range(1, tm_count):
            run.append(run[-1] + counted[frame])
        run = jnp.stack(run)
        row = half_count * ROWS + lax.broadcasted_iota(jnp.int32, (own_rows, both_rows), 0)
        col = lax.broadcasted_iota(jnp.int32, (own_rows, both_rows), 1)
        counts = (row % ROWS == col % ROWS) & (col // ROWS <= row // ROWS)
        counts = counts & (col >= (1 - half) * own_rows)
        for turn in range(turns):
            total = run[:, turn].reshape(both_rows, SHARED_HEADS)
            total_t = jnp.transpose(total)
            steps_t = jnp.transpose(steps[:, turn].reshape(both_rows, SHARED_HEADS))
            for head in all_heads:
                gap = total_t[head : head + 1, :] - total[own_rows:, head : head + 1]
                decay = jnp.exp(jnp.where(counts, gap * rates_ref[head], -1e30))
                d_buf[turn, head] = decay * steps_t[head : head + 1, :]

    @pl.when(half == 0)
    def _():
        x_buf[:, 0:half_count] = jnp.zeros((turns, half_count, ROWS, channels), BF16)

    chunk_lane = lax.broadcasted_iota(jnp.int32, (rows, HEAD_DIM), 1)
    chunk_slot = chunk_lane % SHARED_HEADS

    def attend_for(c, step):
        query_out(c, step).wait_recv()
        owner = lax.rem(chip - step + chips, chips) * 2 + core
        query = qr_buf[step - 1, c].reshape(rows, channels)
        summed, top, total = attend(
            lambda h: query[:, lanes_of(h)], key_of, value_of, bias_of(owner), all_heads
        )
        for h, values in zip(all_heads, summed):
            ps_buf[step - 1, c, :, lanes_of(h)] = values.astype(BF16)
        tops = packed(top, all_heads, chunk_slot, jnp.zeros((rows, HEAD_DIM), F32))
        totals = packed(total, all_heads, chunk_slot, jnp.ones((rows, HEAD_DIM), F32))
        logs = tops + jnp.log2(totals)
        big = logs.astype(BF16)
        rest = logs - big.astype(F32)
        middle = rest.astype(BF16)
        small = (rest - middle.astype(F32)).astype(BF16)
        extra = jnp.where(
            chunk_lane < SHARED_HEADS,
            big.astype(F32),
            jnp.where(chunk_lane < 2 * SHARED_HEADS, middle.astype(F32), small.astype(F32)),
        )
        ps_buf[step - 1, c, :, channels : channels + EXTRA] = extra.astype(BF16)
        partial_out(c, step).start()

    def rows_out(group, turn, peer):
        return remote(
            n_buf.at[turn, group],
            x_buf.at[turn, half_count + place],
            a_send.at[turn, group],
            a_recv.at[turn, place],
            "tm",
            half * half_count + peer,
        )

    def rows_later(group, turn, peer):
        return remote(
            n_buf.at[turn, group],
            x_buf.at[turn, place],
            l_send.at[turn, group],
            l_recv.at[turn, place],
            "tm",
            half_count + peer,
        )

    def rows_in(turn, sender):
        return remote(
            n_buf.at[turn, 0],
            x_buf.at[turn, half_count + sender],
            a_send.at[turn, 0],
            a_recv.at[turn, sender],
            "tm",
            half * half_count + sender,
        )

    def earlier_in(turn, sender):
        return remote(
            n_buf.at[turn, 0],
            x_buf.at[turn, sender],
            l_send.at[turn, 0],
            l_recv.at[turn, sender],
            "tm",
            sender,
        )

    def rows_home(turn):
        return pltpu.make_async_copy(
            n_buf.at[turn, place], x_buf.at[turn, half_count + place], self_sem.at[turn]
        )

    def merge(c):
        turn, first = chunk_groups(c)
        loop(1, chips, lambda step: partial_out(c, step).wait_recv())
        logs = [ll_buf[pl.ds(first, per_chunk), turn].reshape(rows, HEAD_DIM)]
        for step in range(1, chips):
            extra = pr_buf[step - 1, c, :, channels : channels + EXTRA].astype(F32)
            once = pltpu.roll(extra, EXTRA - SHARED_HEADS, 1)
            twice = pltpu.roll(extra, EXTRA - 2 * SHARED_HEADS, 1)
            logs.append(extra + (once + twice))
        top = functools.reduce(jnp.maximum, logs)
        shares = [jnp.exp2(log - top) for log in logs]
        total = functools.reduce(jnp.add, shares)
        shares = [share / total for share in shares]
        attended = []
        for h in all_heads:
            value = shares[0][:, h : h + 1] * ol_buf[
                pl.ds(first, per_chunk), turn, :, lanes_of(h)
            ].reshape(rows, HEAD_DIM)
            for step in range(1, chips):
                value = value + shares[step][:, h : h + 1] * pr_buf[
                    step - 1, c, :, lanes_of(h)
                ].astype(F32)
            attended.append(value.astype(BF16).astype(F32))
        squares = functools.reduce(jnp.add, [a * a for a in attended])
        mean = jnp.sum(squares, axis=-1, keepdims=True) / channels
        scale = lax.rsqrt(mean + 1e-05)
        for h in all_heads:
            normed = attended[h] * scale * pre_ref[:, lanes_of(h)]
            n_buf[turn, pl.ds(first, per_chunk), :, lanes_of(h)] = normed.reshape(
                per_chunk, ROWS, HEAD_DIM
            ).astype(BF16)
        for index in range(per_chunk):
            peer = first + index

            @pl.when(half == 0)
            def _():
                rows_later(peer, turn, peer).start()

            @pl.when(peer != place)
            def _():
                rows_out(peer, turn, peer).start()

            @pl.when(peer == place)
            def _():
                rows_home(turn).start()

    def result_out(turn, step):
        peer = lax.rem(place + step, half_count)
        return remote(
            o_buf.at[turn, peer],
            out_ref.at[place, turn],
            o_send.at[turn, step],
            o_recv.at[turn, step],
            "tm",
            half * half_count + peer,
        )

    def result_in(turn, step):
        sender = lax.rem(place - step + half_count, half_count)
        return remote(
            o_buf.at[turn, sender],
            out_ref.at[sender, turn],
            o_send.at[turn, step],
            o_recv.at[turn, step],
            "tm",
            half * half_count + sender,
        )

    def result_home(turn):
        return pltpu.make_async_copy(
            o_buf.at[turn, place], out_ref.at[place, turn], home_sem.at[turn]
        )

    def mix(turn):
        def take(step):
            rows_in(turn, lax.rem(place - step + half_count, half_count)).wait_recv()

        loop(1, half_count, take)
        rows_home(turn).wait()

        @pl.when(half == 1)
        def _():
            loop(0, half_count, lambda sender: earlier_in(turn, sender).wait_recv())

        values = x_buf[turn].reshape(both_rows, channels)
        across = (((1,), (1,)), ((), ()))
        b_in = lax.dot_general(values, w_in_ref[...], across, preferred_element_type=F32)
        c_out = lax.dot_general(
            values[own_rows:], w_out_ref[...], across, preferred_element_type=F32
        )
        gram = lax.dot_general(c_out, b_in, across, precision=HIGH, preferred_element_type=F32)
        mixing = [(gram * d_buf[turn, h]).astype(BF16) for h in all_heads]
        mixed = [
            jnp.dot(m, values[:, lanes_of(h)], preferred_element_type=F32)
            for m, h in zip(mixing, all_heads)
        ]
        mixed = [
            m + skips_ref[h] * values[own_rows:, lanes_of(h)].astype(F32)
            for m, h in zip(mixed, all_heads)
        ]
        squares = functools.reduce(jnp.add, [m * m for m in mixed])
        mean = jnp.sum(squares, axis=-1, keepdims=True) / channels
        scale = lax.rsqrt(mean + 1e-05)
        for h in all_heads:
            result = mixed[h] * scale * post_ref[:, lanes_of(h)]
            o_buf[turn, :, :, lanes_of(h)] = result.reshape(half_count, ROWS, HEAD_DIM).astype(BF16)
        loop(1, half_count, lambda step: result_out(turn, step).start())
        result_home(turn).start()

    def turn_of_loop(i):
        @pl.when(i + AHEAD < chunks)
        def _():
            send_query(i + AHEAD)

        @pl.when(i < chunks)
        def _():
            loop(1, chips, lambda step: attend_for(i, step))

        @pl.when((i >= LAG_MERGE) & (i < chunks + LAG_MERGE))
        def _():
            merge(i - LAG_MERGE)

        @pl.when(i == LAG_MIX - 1)
        def _():
            make_decays()

        c = i - LAG_MIX
        turn, first = chunk_groups(jnp.maximum(c, 0))

        @pl.when((c >= 0) & (place >= first) & (place < first + per_chunk))
        def _():
            mix(turn)

    loop(0, chunks + LAG_MIX, turn_of_loop)

    for part in range(KV_PARTS):
        for which in range(2):
            partner_kv(which, part).wait_send()
    for which in range(2):
        target = which * half_count + tm // 2

        @pl.when(target != tm)
        def _():
            step_copy(which, target, tm % 2).wait_send()

    def sent_chunk(c):
        def sent(step):
            query_out(c, step).wait_send()
            partial_out(c, step).wait_send()

        loop(1, chips, sent)

    loop(0, chunks, sent_chunk)

    for turn in range(turns):

        def sent_rows(group):
            @pl.when(half == 0)
            def _():
                rows_later(group, turn, group).wait_send()

            @pl.when(group != place)
            def _():
                rows_out(group, turn, group).wait_send()

        loop(0, half_count, sent_rows)

    for turn in range(turns):

        def finish(step):
            result_out(turn, step).wait_send()
            result_in(turn, step).wait_recv()

        loop(1, half_count, finish)
        result_home(turn).wait()


def body(
    queries,
    key_vectors,
    value_vectors,
    block_lists,
    step_sizes,
    decay_rates,
    skip_gains,
    pre_gain,
    state_in_weight,
    state_out_weight,
    post_gain,
):
    tokens, channels = queries.shape[1], queries.shape[2]
    space_count = lax.axis_size("space")
    tm_count = lax.axis_size("tm")
    half_count = tm_count // 2
    turns = tokens // (half_count * ROWS)
    chips = space_count // 2
    chunks = half_count * turns // PER_CHUNK
    rows = PER_CHUNK * ROWS
    state = state_in_weight.shape[1]
    hbm = pl.BlockSpec(memory_space=pl.ANY)
    dma = pltpu.SemaphoreType.DMA
    out = pl.pallas_call(
        functools.partial(kernel, (space_count, tm_count, block_lists.shape[1])),
        out_shape=jax.ShapeDtypeStruct((half_count, turns, ROWS, channels), BF16),
        in_specs=[hbm] * 11,
        out_specs=hbm,
        scratch_shapes=[
            pltpu.SMEM(block_lists.shape, jnp.int32),
            pltpu.SMEM(decay_rates.shape, F32),
            pltpu.SMEM(skip_gains.shape, F32),
            pltpu.VMEM((half_count, turns, ROWS, channels), BF16),
            pltpu.VMEM((tm_count, 2, tokens // tm_count, SHARED_HEADS), F32),
            pltpu.VMEM((1, channels), F32),
            pltpu.VMEM((state, channels), BF16),
            pltpu.VMEM((state, channels), BF16),
            pltpu.VMEM((1, channels), F32),
            pltpu.VMEM((2, 2, tokens, channels), BF16),
            pltpu.VMEM((chips - 1, chunks, PER_CHUNK, ROWS, channels), BF16),
            pltpu.VMEM((chips - 1, chunks, rows, channels + EXTRA), BF16),
            pltpu.VMEM((chips - 1, chunks, rows, channels + EXTRA), BF16),
            pltpu.VMEM((half_count, turns, ROWS, channels), F32),
            pltpu.VMEM((half_count, turns, ROWS, HEAD_DIM), F32),
            pltpu.VMEM((turns, half_count, ROWS, channels), BF16),
            pltpu.VMEM((turns, tm_count, ROWS, channels), BF16),
            pltpu.VMEM((turns, half_count, ROWS, channels), BF16),
            pltpu.VMEM((turns, SHARED_HEADS, half_count * ROWS, tm_count * ROWS), F32),
            dma((8,)),
            dma((2, KV_PARTS)),
            dma((2, KV_PARTS)),
            dma((2, KV_PARTS)),
            dma((2,)),
            dma((2,)),
            dma((2,)),
            dma((chips - 1, chunks)),
            dma((chips - 1, chunks)),
            dma((chips - 1, chunks)),
            dma((chips - 1, chunks)),
            dma((turns, half_count)),
            dma((turns, half_count)),
            dma((turns, half_count)),
            dma((turns, half_count)),
            dma((turns, half_count)),
            dma((turns, half_count)),
            dma((turns,)),
            dma((turns,)),
            pltpu.SemaphoreType.REGULAR,
        ],
        compiler_params=pltpu.CompilerParams(
            collective_id=0, has_side_effects=True, vmem_limit_bytes=VMEM_BYTES
        ),
        name="attend_and_mix",
    )(
        *(
            pltpu.with_memory_space_constraint(operand, pltpu.HBM)
            for operand in (
                block_lists,
                decay_rates,
                skip_gains,
                queries.reshape(half_count, turns, ROWS, channels),
                key_vectors.reshape(tokens, channels),
                value_vectors.reshape(tokens, channels),
                step_sizes,
                pre_gain.reshape(1, channels),
                state_in_weight.T,
                state_out_weight.T,
                post_gain.reshape(1, channels),
            )
        )
    )
    return out.reshape(1, tokens, channels)


def solution(mesh):
    placed = (
        P("tm", "space", None),
        P("tm", "space", None),
        P("tm", "space", None),
        P(),
        P(None, ("space", "tm"), None),
        P(),
        P(),
        P(),
        P(),
        P(),
        P(),
    )
    return jax.shard_map(
        body, mesh=mesh, in_specs=placed, out_specs=P("tm", "space", None), check_vma=False
    )
```

```python
import functools
import math

import jax
import jax.numpy as jnp
from jax import lax
from jax.experimental import pallas as pl
from jax.experimental.pallas import tpu as pltpu
from jax.sharding import PartitionSpec as P

SHARED_HEADS = 16
HEAD_DIM = 128
ROWS = 8
PER_CHUNK = 1
AHEAD = (6, 4)
LAG_MERGE = (4, 3)
LAG_MIX = (8, 7)
KV_PARTS = 2
EXTRA = 128
VMEM_BYTES = 44 * 1024 * 1024
MESH = pl.DeviceIdType.MESH
F32 = jnp.float32
BF16 = jnp.bfloat16
HIGH = lax.Precision.HIGHEST


def remote(src, dst, send_sem, recv_sem, axis, index):
    return pltpu.make_async_remote_copy(
        src_ref=src,
        dst_ref=dst,
        send_sem=send_sem,
        recv_sem=recv_sem,
        device_id={axis: index},
        device_id_type=MESH,
    )


def loop(low, high, act):
    if high - low == 1:
        act(low)
    elif high > low:

        def turn(i, carry):
            act(i)
            return carry

        lax.fori_loop(low, high, turn, 0)


def lanes_of(head):
    return slice(head * HEAD_DIM, (head + 1) * HEAD_DIM)


def attend(query, key, value, bias, heads):
    factor = math.log2(math.e) / math.sqrt(HEAD_DIM)
    across = (((1,), (1,)), ((), ()))
    scores = [
        lax.dot_general(query(h), key(h), across, preferred_element_type=F32) * factor + bias
        for h in heads
    ]
    tops = [jnp.max(s, axis=-1, keepdims=True) for s in scores]
    weights = [jnp.exp2(s - m) for s, m in zip(scores, tops)]
    totals = [jnp.sum(w, axis=-1, keepdims=True) for w in weights]
    sums = [
        jnp.dot(w.astype(BF16), value(h), preferred_element_type=F32) for w, h in zip(weights, heads)
    ]
    return [s / t for s, t in zip(sums, totals)], tops, totals


def packed(columns, heads, lane, into):
    for h, column in zip(heads, columns):
        into = jnp.where(lane == h, column, into)
    return into


def kernel(
    dims,
    lists_hbm,
    rates_hbm,
    skips_hbm,
    q_hbm,
    k_hbm,
    v_hbm,
    steps_hbm,
    pre_hbm,
    w_in_hbm,
    w_out_hbm,
    post_hbm,
    out_ref,
    lists_ref,
    rates_ref,
    skips_ref,
    q_ref,
    steps_ref,
    pre_ref,
    w_in_ref,
    w_out_ref,
    post_ref,
    kv_buf,
    qr_buf,
    ps_buf,
    pr_buf,
    ol_buf,
    ll_buf,
    n_buf,
    x_buf,
    o_buf,
    d_buf,
    load_sem,
    own_sem,
    kv_send,
    kv_recv,
    step_send,
    step_recv,
    step_own,
    q_send,
    q_recv,
    p_send,
    p_recv,
    a_send,
    a_recv,
    l_send,
    l_recv,
    o_send,
    o_recv,
    self_sem,
    home_sem,
    ready_sem,
):
    space_count, tm_count, list_width = dims
    half_count, turns, _, channels = q_hbm.shape
    tokens = half_count * turns * ROWS
    per_chunk = PER_CHUNK
    sets = half_count // per_chunk
    chunks = sets * turns
    rows = per_chunk * ROWS
    chips = space_count // 2
    all_heads = range(SHARED_HEADS)
    space = lax.axis_index("space")
    tm = lax.axis_index("tm")
    half = tm // half_count
    place = tm % half_count
    chip = space // 2
    core = space % 2
    partner = chip * 2 + 1 - core
    ahead, lag_merge, lag_mix = (
        pair[1] + (1 - core) * (pair[0] - pair[1]) for pair in (AHEAD, LAG_MERGE, LAG_MIX)
    )

    barrier = pltpu.get_barrier_semaphore()

    def greet_chip(step):
        peer = lax.rem(chip + step, chips) * 2 + core
        pl.semaphore_signal(barrier, inc=1, device_id={"space": peer}, device_id_type=MESH)

    def greet_frame(peer):
        pl.semaphore_signal(barrier, inc=1, device_id={"tm": peer}, device_id_type=MESH)

    def answer_frame(peer):
        pl.semaphore_signal(ready_sem, inc=1, device_id={"tm": peer}, device_id_type=MESH)

    pl.semaphore_signal(barrier, inc=1, device_id={"space": partner}, device_id_type=MESH)
    loop(1, chips, greet_chip)
    lax.fori_loop(tm + 1, tm_count, lambda peer, carry: (greet_frame(peer), carry)[1], 0)

    part_width = channels // KV_PARTS

    def kv_span(part):
        return pl.ds(part * part_width, part_width)

    def own_kv(which, part):
        source = (k_hbm, v_hbm)[which]
        return pltpu.make_async_copy(
            source.at[:, kv_span(part)],
            kv_buf.at[which, core, :, kv_span(part)],
            own_sem.at[which, part],
        )

    def partner_kv(which, part):
        source = (k_hbm, v_hbm)[which]
        return remote(
            source.at[:, kv_span(part)],
            kv_buf.at[which, core, :, kv_span(part)],
            kv_send.at[which, part],
            kv_recv.at[which, part],
            "space",
            partner,
        )

    load_q = pltpu.make_async_copy(q_hbm, q_ref, load_sem.at[0])
    load_q.start()
    for part in range(KV_PARTS):
        for which in range(2):
            own_kv(which, part).start()
    loads = [
        pltpu.make_async_copy(source, target, load_sem.at[1 + index])
        for index, (source, target) in enumerate(
            (
                (lists_hbm, lists_ref),
                (rates_hbm, rates_ref),
                (skips_hbm, skips_ref),
                (pre_hbm, pre_ref),
                (w_in_hbm, w_in_ref),
                (w_out_hbm, w_out_ref),
                (post_hbm, post_ref),
            )
        )
    ]
    for load in loads:
        load.start()

    def chunk_groups(c):
        return c // sets, (sets - 1 - c % sets) * per_chunk

    def query_out(c, step):
        turn, first = chunk_groups(c)
        return remote(
            q_hbm.at[pl.ds(first, per_chunk), turn],
            qr_buf.at[step - 1, c],
            q_send.at[step - 1, c],
            q_recv.at[step - 1, c],
            "space",
            lax.rem(chip + step, chips) * 2 + core,
        )

    def partial_out(c, step):
        return remote(
            ps_buf.at[step - 1, c],
            pr_buf.at[step - 1, c],
            p_send.at[step - 1, c],
            p_recv.at[step - 1, c],
            "space",
            lax.rem(chip - step + chips, chips) * 2 + core,
        )

    def send_query(c):
        loop(1, chips, lambda step: query_out(c, step).start())

    pl.semaphore_wait(barrier, chips + tm)

    send_query(0)
    for part in range(KV_PARTS):
        for which in range(2):
            partner_kv(which, part).start()
    lax.fori_loop(1, jnp.minimum(ahead, chunks), lambda c, carry: (send_query(c), carry)[1], 0)
    lax.fori_loop(0, tm, lambda peer, carry: (answer_frame(peer), carry)[1], 0)

    def step_copy(which, target, part):
        return remote(
            steps_hbm,
            steps_ref.at[:, part],
            step_send.at[which],
            step_recv.at[part],
            "tm",
            target,
        )

    def step_local(part):
        return pltpu.make_async_copy(steps_hbm, steps_ref.at[:, part], step_own.at[part])

    for load in loads:
        load.wait()
    load_q.wait()

    def key_of(h):
        return kv_buf[0, :, :, lanes_of(h)].reshape(2 * tokens, HEAD_DIM)

    def value_of(h):
        return kv_buf[1, :, :, lanes_of(h)].reshape(2 * tokens, HEAD_DIM)

    block_of = chip * 2 + lax.broadcasted_iota(jnp.int32, (1, 2 * tokens), 1) // tokens

    def bias_of(owner):
        chosen = block_of == lists_ref[owner, 0]
        for entry in range(1, list_width):
            chosen = chosen | (block_of == lists_ref[owner, entry])
        return jnp.where(chosen, 0.0, -1e30).astype(F32)

    own_rows = half_count * ROWS
    both_rows = tm_count * ROWS

    def send_steps():
        @pl.when(tm < tm_count - 1)
        def _():
            pl.semaphore_wait(ready_sem, tm_count - 1 - tm)

        for which in range(2):
            target = which * half_count + tm // 2
            part = tm % 2

            @pl.when(target != tm)
            def _():
                step_copy(which, target, part).start()

            @pl.when(target == tm)
            def _():
                step_local(part).start()

    def make_decays():
        for part in range(2):
            origin = 2 * place + part

            @pl.when(origin != tm)
            def _():
                step_copy(0, origin, part).wait_recv()

            @pl.when(origin == tm)
            def _():
                step_local(part).wait()

        steps = steps_ref[...].reshape(tm_count, turns, ROWS, SHARED_HEADS)
        earlier, later = steps[:half_count], steps[half_count:]
        own = jnp.where(half == 1, later, earlier)
        steps = jnp.concatenate([earlier, own], axis=0)
        counted = jnp.concatenate([jnp.where(half == 1, earlier, 0.0), own], axis=0)
        run = [counted[0]]
        for frame in range(1, tm_count):
            run.append(run[-1] + counted[frame])
        run = jnp.stack(run)
        row = half_count * ROWS + lax.broadcasted_iota(jnp.int32, (own_rows, both_rows), 0)
        col = lax.broadcasted_iota(jnp.int32, (own_rows, both_rows), 1)
        counts = (row % ROWS == col % ROWS) & (col // ROWS <= row // ROWS)
        counts = counts & (col >= (1 - half) * own_rows)
        for turn in range(turns):
            total = run[:, turn].reshape(both_rows, SHARED_HEADS)
            total_t = jnp.transpose(total)
            steps_t = jnp.transpose(steps[:, turn].reshape(both_rows, SHARED_HEADS))
            for head in all_heads:
                gap = total_t[head : head + 1, :] - total[own_rows:, head : head + 1]
                decay = jnp.exp(jnp.where(counts, gap * rates_ref[head], -1e30))
                d_buf[turn, head] = decay * steps_t[head : head + 1, :]

    for part in range(KV_PARTS):
        for which in range(2):
            own_kv(which, part).wait()
            partner_kv(which, part).wait_recv()

    @pl.when(half == 0)
    def _():
        x_buf[:, 0:half_count] = jnp.zeros((turns, half_count, ROWS, channels), BF16)

    chunk_lane = lax.broadcasted_iota(jnp.int32, (rows, HEAD_DIM), 1)

    def attend_for(c, step, with_own):
        turn, first = chunk_groups(c)
        query_out(c, step).wait_recv()
        owner = lax.rem(chip - step + chips, chips) * 2 + core
        query = qr_buf[step - 1, c].reshape(rows, channels)
        bias = bias_of(owner)
        skip = rows if with_own else 0
        if with_own:
            mine = q_ref[pl.ds(first, per_chunk), turn].reshape(rows, channels)
            query = jnp.concatenate([mine.astype(F32), query.astype(F32)], axis=0).astype(BF16)
            row_of = lax.broadcasted_iota(jnp.int32, (2 * rows, 2 * tokens), 0)
            bias = jnp.where(row_of < rows, bias_of(space), bias)
        summed, top, total = attend(
            lambda h: query[:, lanes_of(h)], key_of, value_of, bias, all_heads
        )
        slot_of = lax.broadcasted_iota(jnp.int32, (skip + rows, HEAD_DIM), 1) % SHARED_HEADS
        for h, values in zip(all_heads, summed):
            ps_buf[step - 1, c, :, lanes_of(h)] = values[skip:].astype(BF16)
        tops = packed(top, all_heads, slot_of, jnp.zeros((skip + rows, HEAD_DIM), F32))
        totals = packed(total, all_heads, slot_of, jnp.ones((skip + rows, HEAD_DIM), F32))
        both_logs = tops + jnp.log2(totals)
        logs = both_logs[skip:]
        big = logs.astype(BF16)
        rest = logs - big.astype(F32)
        middle = rest.astype(BF16)
        small = (rest - middle.astype(F32)).astype(BF16)
        extra = jnp.where(
            chunk_lane < SHARED_HEADS,
            big.astype(F32),
            jnp.where(chunk_lane < 2 * SHARED_HEADS, middle.astype(F32), small.astype(F32)),
        )
        ps_buf[step - 1, c, :, channels : channels + EXTRA] = extra.astype(BF16)
        partial_out(c, step).start()
        if with_own:
            for h, values in zip(all_heads, summed):
                ol_buf[pl.ds(first, per_chunk), turn, :, lanes_of(h)] = values[:skip].reshape(
                    per_chunk, ROWS, HEAD_DIM
                )
            ll_buf[pl.ds(first, per_chunk), turn] = both_logs[:skip].reshape(
                per_chunk, ROWS, HEAD_DIM
            )

    def rows_out(group, turn, peer):
        return remote(
            n_buf.at[turn, group],
            x_buf.at[turn, half_count + place],
            a_send.at[turn, group],
            a_recv.at[turn, place],
            "tm",
            half * half_count + peer,
        )

    def rows_later(group, turn, peer):
        return remote(
            n_buf.at[turn, group],
            x_buf.at[turn, place],
            l_send.at[turn, group],
            l_recv.at[turn, place],
            "tm",
            half_count + peer,
        )

    def rows_in(turn, sender):
        return remote(
            n_buf.at[turn, 0],
            x_buf.at[turn, half_count + sender],
            a_send.at[turn, 0],
            a_recv.at[turn, sender],
            "tm",
            half * half_count + sender,
        )

    def earlier_in(turn, sender):
        return remote(
            n_buf.at[turn, 0],
            x_buf.at[turn, sender],
            l_send.at[turn, 0],
            l_recv.at[turn, sender],
            "tm",
            sender,
        )

    def rows_home(turn):
        return pltpu.make_async_copy(
            n_buf.at[turn, place], x_buf.at[turn, half_count + place], self_sem.at[turn]
        )

    def merge(c):
        turn, first = chunk_groups(c)
        loop(1, chips, lambda step: partial_out(c, step).wait_recv())
        logs = [ll_buf[pl.ds(first, per_chunk), turn].reshape(rows, HEAD_DIM)]
        for step in range(1, chips):
            extra = pr_buf[step - 1, c, :, channels : channels + EXTRA].astype(F32)
            once = pltpu.roll(extra, EXTRA - SHARED_HEADS, 1)
            twice = pltpu.roll(extra, EXTRA - 2 * SHARED_HEADS, 1)
            logs.append(extra + (once + twice))
        top = functools.reduce(jnp.maximum, logs)
        shares = [jnp.exp2(log - top) for log in logs]
        total = functools.reduce(jnp.add, shares)
        shares = [share / total for share in shares]
        attended = []
        for h in all_heads:
            value = shares[0][:, h : h + 1] * ol_buf[
                pl.ds(first, per_chunk), turn, :, lanes_of(h)
            ].reshape(rows, HEAD_DIM)
            for step in range(1, chips):
                value = value + shares[step][:, h : h + 1] * pr_buf[
                    step - 1, c, :, lanes_of(h)
                ].astype(F32)
            attended.append(value.astype(BF16).astype(F32))
        squares = functools.reduce(jnp.add, [a * a for a in attended])
        mean = jnp.sum(squares, axis=-1, keepdims=True) / channels
        scale = lax.rsqrt(mean + 1e-05)
        for h in all_heads:
            normed = attended[h] * scale * pre_ref[:, lanes_of(h)]
            n_buf[turn, pl.ds(first, per_chunk), :, lanes_of(h)] = normed.reshape(
                per_chunk, ROWS, HEAD_DIM
            ).astype(BF16)
        for index in range(per_chunk):
            peer = first + index

            @pl.when(half == 0)
            def _():
                rows_later(peer, turn, peer).start()

            @pl.when(peer != place)
            def _():
                rows_out(peer, turn, peer).start()

            @pl.when(peer == place)
            def _():
                rows_home(turn).start()

    def result_out(turn, step):
        peer = lax.rem(place + step, half_count)
        return remote(
            o_buf.at[turn, peer],
            out_ref.at[place, turn],
            o_send.at[turn, step],
            o_recv.at[turn, step],
            "tm",
            half * half_count + peer,
        )

    def result_in(turn, step):
        sender = lax.rem(place - step + half_count, half_count)
        return remote(
            o_buf.at[turn, sender],
            out_ref.at[sender, turn],
            o_send.at[turn, step],
            o_recv.at[turn, step],
            "tm",
            half * half_count + sender,
        )

    def result_home(turn):
        return pltpu.make_async_copy(
            o_buf.at[turn, place], out_ref.at[place, turn], home_sem.at[turn]
        )

    def mix(turn):
        def take(step):
            rows_in(turn, lax.rem(place - step + half_count, half_count)).wait_recv()

        loop(1, half_count, take)
        rows_home(turn).wait()

        @pl.when(half == 1)
        def _():
            loop(0, half_count, lambda sender: earlier_in(turn, sender).wait_recv())

        values = x_buf[turn].reshape(both_rows, channels)
        across = (((1,), (1,)), ((), ()))
        b_in = lax.dot_general(values, w_in_ref[...], across, preferred_element_type=F32)
        c_out = lax.dot_general(
            values[own_rows:], w_out_ref[...], across, preferred_element_type=F32
        )
        gram = lax.dot_general(c_out, b_in, across, precision=HIGH, preferred_element_type=F32)
        mixing = [(gram * d_buf[turn, h]).astype(BF16) for h in all_heads]
        mixed = [
            jnp.dot(m, values[:, lanes_of(h)], preferred_element_type=F32)
            for m, h in zip(mixing, all_heads)
        ]
        mixed = [
            m + skips_ref[h] * values[own_rows:, lanes_of(h)].astype(F32)
            for m, h in zip(mixed, all_heads)
        ]
        squares = functools.reduce(jnp.add, [m * m for m in mixed])
        mean = jnp.sum(squares, axis=-1, keepdims=True) / channels
        scale = lax.rsqrt(mean + 1e-05)
        for h in all_heads:
            result = mixed[h] * scale * post_ref[:, lanes_of(h)]
            o_buf[turn, :, :, lanes_of(h)] = result.reshape(half_count, ROWS, HEAD_DIM).astype(BF16)
        loop(1, half_count, lambda step: result_out(turn, step).start())
        result_home(turn).start()

    def turn_of_loop(i):
        @pl.when(i + ahead < chunks)
        def _():
            send_query(i + ahead)

        @pl.when(i < chunks)
        def _():
            attend_for(i, 1, True)
            loop(2, chips, lambda step: attend_for(i, step, False))

        @pl.when((i >= lag_merge) & (i < chunks + lag_merge))
        def _():
            merge(i - lag_merge)

        @pl.when(i == 1)
        def _():
            send_steps()

        @pl.when(i == lag_mix - 1)
        def _():
            make_decays()

        c = i - lag_mix
        turn, first = chunk_groups(jnp.maximum(c, 0))

        @pl.when((c >= 0) & (c < chunks) & (place >= first) & (place < first + per_chunk))
        def _():
            mix(turn)

    loop(0, chunks + max(LAG_MIX), turn_of_loop)

    for part in range(KV_PARTS):
        for which in range(2):
            partner_kv(which, part).wait_send()
    for which in range(2):
        target = which * half_count + tm // 2

        @pl.when(target != tm)
        def _():
            step_copy(which, target, tm % 2).wait_send()

    def sent_chunk(c):
        def sent(step):
            query_out(c, step).wait_send()
            partial_out(c, step).wait_send()

        loop(1, chips, sent)

    loop(0, chunks, sent_chunk)

    for turn in range(turns):

        def sent_rows(group):
            @pl.when(half == 0)
            def _():
                rows_later(group, turn, group).wait_send()

            @pl.when(group != place)
            def _():
                rows_out(group, turn, group).wait_send()

        loop(0, half_count, sent_rows)

    for turn in range(turns):

        def finish(step):
            result_out(turn, step).wait_send()
            result_in(turn, step).wait_recv()

        loop(1, half_count, finish)
        result_home(turn).wait()


def body(
    queries,
    key_vectors,
    value_vectors,
    block_lists,
    step_sizes,
    decay_rates,
    skip_gains,
    pre_gain,
    state_in_weight,
    state_out_weight,
    post_gain,
):
    tokens, channels = queries.shape[1], queries.shape[2]
    space_count = lax.axis_size("space")
    tm_count = lax.axis_size("tm")
    half_count = tm_count // 2
    turns = tokens // (half_count * ROWS)
    chips = space_count // 2
    chunks = half_count * turns // PER_CHUNK
    rows = PER_CHUNK * ROWS
    state = state_in_weight.shape[1]
    hbm = pl.BlockSpec(memory_space=pl.ANY)
    dma = pltpu.SemaphoreType.DMA
    out = pl.pallas_call(
        functools.partial(kernel, (space_count, tm_count, block_lists.shape[1])),
        out_shape=jax.ShapeDtypeStruct((half_count, turns, ROWS, channels), BF16),
        in_specs=[hbm] * 11,
        out_specs=hbm,
        scratch_shapes=[
            pltpu.SMEM(block_lists.shape, jnp.int32),
            pltpu.SMEM(decay_rates.shape, F32),
            pltpu.SMEM(skip_gains.shape, F32),
            pltpu.VMEM((half_count, turns, ROWS, channels), BF16),
            pltpu.VMEM((tm_count, 2, tokens // tm_count, SHARED_HEADS), F32),
            pltpu.VMEM((1, channels), F32),
            pltpu.VMEM((state, channels), BF16),
            pltpu.VMEM((state, channels), BF16),
            pltpu.VMEM((1, channels), F32),
            pltpu.VMEM((2, 2, tokens, channels), BF16),
            pltpu.VMEM((chips - 1, chunks, PER_CHUNK, ROWS, channels), BF16),
            pltpu.VMEM((chips - 1, chunks, rows, channels + EXTRA), BF16),
            pltpu.VMEM((chips - 1, chunks, rows, channels + EXTRA), BF16),
            pltpu.VMEM((half_count, turns, ROWS, channels), F32),
            pltpu.VMEM((half_count, turns, ROWS, HEAD_DIM), F32),
            pltpu.VMEM((turns, half_count, ROWS, channels), BF16),
            pltpu.VMEM((turns, tm_count, ROWS, channels), BF16),
            pltpu.VMEM((turns, half_count, ROWS, channels), BF16),
            pltpu.VMEM((turns, SHARED_HEADS, half_count * ROWS, tm_count * ROWS), F32),
            dma((8,)),
            dma((2, KV_PARTS)),
            dma((2, KV_PARTS)),
            dma((2, KV_PARTS)),
            dma((2,)),
            dma((2,)),
            dma((2,)),
            dma((chips - 1, chunks)),
            dma((chips - 1, chunks)),
            dma((chips - 1, chunks)),
            dma((chips - 1, chunks)),
            dma((turns, half_count)),
            dma((turns, half_count)),
            dma((turns, half_count)),
            dma((turns, half_count)),
            dma((turns, half_count)),
            dma((turns, half_count)),
            dma((turns,)),
            dma((turns,)),
            pltpu.SemaphoreType.REGULAR,
        ],
        compiler_params=pltpu.CompilerParams(
            collective_id=0, has_side_effects=True, vmem_limit_bytes=VMEM_BYTES
        ),
        name="attend_and_mix",
    )(
        *(
            pltpu.with_memory_space_constraint(operand, pltpu.HBM)
            for operand in (
                block_lists,
                decay_rates,
                skip_gains,
                queries.reshape(half_count, turns, ROWS, channels),
                key_vectors.reshape(tokens, channels),
                value_vectors.reshape(tokens, channels),
                step_sizes,
                pre_gain.reshape(1, channels),
                state_in_weight.T,
                state_out_weight.T,
                post_gain.reshape(1, channels),
            )
        )
    )
    return out.reshape(1, tokens, channels)


def solution(mesh):
    placed = (
        P("tm", "space", None),
        P("tm", "space", None),
        P("tm", "space", None),
        P(),
        P(None, ("space", "tm"), None),
        P(),
        P(),
        P(),
        P(),
        P(),
        P(),
    )
    return jax.shard_map(
        body, mesh=mesh, in_specs=placed, out_specs=P("tm", "space", None), check_vma=False
    )
```

```python
import functools
import math

import jax
import jax.numpy as jnp
from jax import lax
from jax.experimental import pallas as pl
from jax.experimental.pallas import tpu as pltpu
from jax.sharding import PartitionSpec as P

SHARED_HEADS = 16
HEAD_DIM = 128
ROWS = 8
PER_CHUNK = 1
AHEAD = (5, 5)
LAG_MERGE = (4, 3)
LAG_MIX = (8, 7)
KV_PARTS = 1
EXTRA = 128
VMEM_BYTES = 44 * 1024 * 1024
MESH = pl.DeviceIdType.MESH
F32 = jnp.float32
BF16 = jnp.bfloat16
HIGH = lax.Precision.HIGHEST


def remote(src, dst, send_sem, recv_sem, axis, index):
    return pltpu.make_async_remote_copy(
        src_ref=src,
        dst_ref=dst,
        send_sem=send_sem,
        recv_sem=recv_sem,
        device_id={axis: index},
        device_id_type=MESH,
    )


def loop(low, high, act):
    if high - low == 1:
        act(low)
    elif high > low:

        def turn(i, carry):
            act(i)
            return carry

        lax.fori_loop(low, high, turn, 0)


def lanes_of(head):
    return slice(head * HEAD_DIM, (head + 1) * HEAD_DIM)


def attend(query, key, value, bias, heads):
    factor = math.log2(math.e) / math.sqrt(HEAD_DIM)
    across = (((1,), (1,)), ((), ()))
    scores = [
        lax.dot_general(query(h), key(h), across, preferred_element_type=F32) * factor + bias
        for h in heads
    ]
    tops = [jnp.max(s, axis=-1, keepdims=True) for s in scores]
    weights = [jnp.exp2(s - m) for s, m in zip(scores, tops)]
    totals = [jnp.sum(w, axis=-1, keepdims=True) for w in weights]
    sums = [
        jnp.dot(w.astype(BF16), value(h), preferred_element_type=F32) for w, h in zip(weights, heads)
    ]
    return [s / t for s, t in zip(sums, totals)], tops, totals


def packed(columns, heads, lane, into):
    for h, column in zip(heads, columns):
        into = jnp.where(lane == h, column, into)
    return into


def kernel(
    dims,
    lists_hbm,
    rates_hbm,
    skips_hbm,
    q_hbm,
    k_hbm,
    v_hbm,
    steps_hbm,
    pre_hbm,
    w_in_hbm,
    w_out_hbm,
    post_hbm,
    out_ref,
    lists_ref,
    rates_ref,
    skips_ref,
    q_ref,
    steps_ref,
    pre_ref,
    w_in_ref,
    w_out_ref,
    post_ref,
    kv_buf,
    qr_buf,
    ps_buf,
    pr_buf,
    ol_buf,
    ll_buf,
    n_buf,
    x_buf,
    o_buf,
    d_buf,
    load_sem,
    own_sem,
    kv_send,
    kv_recv,
    step_send,
    step_recv,
    step_own,
    q_send,
    q_recv,
    p_send,
    p_recv,
    a_send,
    a_recv,
    l_send,
    l_recv,
    o_send,
    o_recv,
    self_sem,
    home_sem,
    ready_sem,
):
    space_count, tm_count, list_width = dims
    half_count, turns, _, channels = q_hbm.shape
    tokens = half_count * turns * ROWS
    per_chunk = PER_CHUNK
    sets = half_count // per_chunk
    chunks = sets * turns
    rows = per_chunk * ROWS
    chips = space_count // 2
    all_heads = range(SHARED_HEADS)
    space = lax.axis_index("space")
    tm = lax.axis_index("tm")
    half = tm // half_count
    place = tm % half_count
    chip = space // 2
    core = space % 2
    partner = chip * 2 + 1 - core
    ahead, lag_merge, lag_mix = (
        pair[1] + (1 - core) * (pair[0] - pair[1]) for pair in (AHEAD, LAG_MERGE, LAG_MIX)
    )

    barrier = pltpu.get_barrier_semaphore()

    def greet_chip(step):
        peer = lax.rem(chip + step, chips) * 2 + 1 - core
        pl.semaphore_signal(barrier, inc=1, device_id={"space": peer}, device_id_type=MESH)

    def greet_frame(peer):
        pl.semaphore_signal(barrier, inc=1, device_id={"tm": peer}, device_id_type=MESH)

    def answer_frame(peer):
        pl.semaphore_signal(ready_sem, inc=1, device_id={"tm": peer}, device_id_type=MESH)

    pl.semaphore_signal(barrier, inc=1, device_id={"space": partner}, device_id_type=MESH)
    loop(1, chips, greet_chip)
    lax.fori_loop(tm + 1, tm_count, lambda peer, carry: (greet_frame(peer), carry)[1], 0)

    part_width = channels // KV_PARTS

    def kv_span(part):
        return pl.ds(part * part_width, part_width)

    def own_kv(which, part):
        source = (k_hbm, v_hbm)[which]
        return pltpu.make_async_copy(
            source.at[:, kv_span(part)],
            kv_buf.at[which, core, :, kv_span(part)],
            own_sem.at[which, part],
        )

    def partner_kv(which, part):
        source = (k_hbm, v_hbm)[which]
        return remote(
            source.at[:, kv_span(part)],
            kv_buf.at[which, core, :, kv_span(part)],
            kv_send.at[which, part],
            kv_recv.at[which, part],
            "space",
            partner,
        )

    load_q = pltpu.make_async_copy(q_hbm, q_ref, load_sem.at[0])
    load_q.start()
    for part in range(KV_PARTS):
        for which in range(2):
            own_kv(which, part).start()
    loads = [
        pltpu.make_async_copy(source, target, load_sem.at[1 + index])
        for index, (source, target) in enumerate(
            (
                (lists_hbm, lists_ref),
                (rates_hbm, rates_ref),
                (skips_hbm, skips_ref),
                (pre_hbm, pre_ref),
                (w_in_hbm, w_in_ref),
                (w_out_hbm, w_out_ref),
                (post_hbm, post_ref),
            )
        )
    ]
    for load in loads:
        load.start()

    def chunk_groups(c):
        return c // sets, (sets - 1 - c % sets) * per_chunk

    def query_out(c, step):
        turn, first = chunk_groups(c)
        return remote(
            q_hbm.at[pl.ds(first, per_chunk), turn],
            qr_buf.at[step - 1, c],
            q_send.at[step - 1, c],
            q_recv.at[step - 1, c],
            "space",
            lax.rem(chip + step, chips) * 2 + 1 - core,
        )

    def partial_out(c, step):
        return remote(
            ps_buf.at[step - 1, c],
            pr_buf.at[step - 1, c],
            p_send.at[step - 1, c],
            p_recv.at[step - 1, c],
            "space",
            lax.rem(chip - step + chips, chips) * 2 + 1 - core,
        )

    def send_query(c):
        loop(1, chips, lambda step: query_out(c, step).start())

    pl.semaphore_wait(barrier, chips + tm)

    send_query(0)
    for part in range(KV_PARTS):
        for which in range(2):
            partner_kv(which, part).start()
    lax.fori_loop(1, jnp.minimum(ahead, chunks), lambda c, carry: (send_query(c), carry)[1], 0)
    lax.fori_loop(0, tm, lambda peer, carry: (answer_frame(peer), carry)[1], 0)

    def step_copy(which, target, part):
        return remote(
            steps_hbm,
            steps_ref.at[:, part],
            step_send.at[which],
            step_recv.at[part],
            "tm",
            target,
        )

    def step_local(part):
        return pltpu.make_async_copy(steps_hbm, steps_ref.at[:, part], step_own.at[part])

    for load in loads:
        load.wait()
    load_q.wait()

    def key_of(h):
        return kv_buf[0, :, :, lanes_of(h)].reshape(2 * tokens, HEAD_DIM)

    def value_of(h):
        return kv_buf[1, :, :, lanes_of(h)].reshape(2 * tokens, HEAD_DIM)

    block_of = chip * 2 + lax.broadcasted_iota(jnp.int32, (1, 2 * tokens), 1) // tokens

    def bias_of(owner):
        chosen = block_of == lists_ref[owner, 0]
        for entry in range(1, list_width):
            chosen = chosen | (block_of == lists_ref[owner, entry])
        return jnp.where(chosen, 0.0, -1e30).astype(F32)

    own_rows = half_count * ROWS
    both_rows = tm_count * ROWS

    def send_steps():
        @pl.when(tm < tm_count - 1)
        def _():
            pl.semaphore_wait(ready_sem, tm_count - 1 - tm)

        for which in range(2):
            target = which * half_count + tm // 2
            part = tm % 2

            @pl.when(target != tm)
            def _():
                step_copy(which, target, part).start()

            @pl.when(target == tm)
            def _():
                step_local(part).start()

    def make_decays():
        for part in range(2):
            origin = 2 * place + part

            @pl.when(origin != tm)
            def _():
                step_copy(0, origin, part).wait_recv()

            @pl.when(origin == tm)
            def _():
                step_local(part).wait()

        steps = steps_ref[...].reshape(tm_count, turns, ROWS, SHARED_HEADS)
        earlier, later = steps[:half_count], steps[half_count:]
        own = jnp.where(half == 1, later, earlier)
        steps = jnp.concatenate([earlier, own], axis=0)
        counted = jnp.concatenate([jnp.where(half == 1, earlier, 0.0), own], axis=0)
        run = [counted[0]]
        for frame in range(1, tm_count):
            run.append(run[-1] + counted[frame])
        run = jnp.stack(run)
        row = half_count * ROWS + lax.broadcasted_iota(jnp.int32, (own_rows, both_rows), 0)
        col = lax.broadcasted_iota(jnp.int32, (own_rows, both_rows), 1)
        counts = (row % ROWS == col % ROWS) & (col // ROWS <= row // ROWS)
        counts = counts & (col >= (1 - half) * own_rows)
        for turn in range(turns):
            total = run[:, turn].reshape(both_rows, SHARED_HEADS)
            total_t = jnp.transpose(total)
            steps_t = jnp.transpose(steps[:, turn].reshape(both_rows, SHARED_HEADS))
            for head in all_heads:
                gap = total_t[head : head + 1, :] - total[own_rows:, head : head + 1]
                decay = jnp.exp(jnp.where(counts, gap * rates_ref[head], -1e30))
                d_buf[turn, head] = decay * steps_t[head : head + 1, :]

    for part in range(KV_PARTS):
        for which in range(2):
            own_kv(which, part).wait()
            partner_kv(which, part).wait_recv()

    @pl.when(half == 0)
    def _():
        x_buf[:, 0:half_count] = jnp.zeros((turns, half_count, ROWS, channels), BF16)

    chunk_lane = lax.broadcasted_iota(jnp.int32, (rows, HEAD_DIM), 1)

    def attend_for(c, step, with_own):
        turn, first = chunk_groups(c)
        query_out(c, step).wait_recv()
        owner = lax.rem(chip - step + chips, chips) * 2 + 1 - core
        query = qr_buf[step - 1, c].reshape(rows, channels)
        bias = bias_of(owner)
        skip = rows if with_own else 0
        if with_own:
            mine = q_ref[pl.ds(first, per_chunk), turn].reshape(rows, channels)
            query = jnp.concatenate([mine.astype(F32), query.astype(F32)], axis=0).astype(BF16)
            row_of = lax.broadcasted_iota(jnp.int32, (2 * rows, 2 * tokens), 0)
            bias = jnp.where(row_of < rows, bias_of(space), bias)
        summed, top, total = attend(
            lambda h: query[:, lanes_of(h)], key_of, value_of, bias, all_heads
        )
        slot_of = lax.broadcasted_iota(jnp.int32, (skip + rows, HEAD_DIM), 1) % SHARED_HEADS
        for h, values in zip(all_heads, summed):
            ps_buf[step - 1, c, :, lanes_of(h)] = values[skip:].astype(BF16)
        tops = packed(top, all_heads, slot_of, jnp.zeros((skip + rows, HEAD_DIM), F32))
        totals = packed(total, all_heads, slot_of, jnp.ones((skip + rows, HEAD_DIM), F32))
        both_logs = tops + jnp.log2(totals)
        logs = both_logs[skip:]
        big = logs.astype(BF16)
        rest = logs - big.astype(F32)
        middle = rest.astype(BF16)
        small = (rest - middle.astype(F32)).astype(BF16)
        extra = jnp.where(
            chunk_lane < SHARED_HEADS,
            big.astype(F32),
            jnp.where(chunk_lane < 2 * SHARED_HEADS, middle.astype(F32), small.astype(F32)),
        )
        ps_buf[step - 1, c, :, channels : channels + EXTRA] = extra.astype(BF16)
        partial_out(c, step).start()
        if with_own:
            for h, values in zip(all_heads, summed):
                ol_buf[pl.ds(first, per_chunk), turn, :, lanes_of(h)] = values[:skip].reshape(
                    per_chunk, ROWS, HEAD_DIM
                )
            ll_buf[pl.ds(first, per_chunk), turn] = both_logs[:skip].reshape(
                per_chunk, ROWS, HEAD_DIM
            )

    def rows_out(group, turn, peer):
        return remote(
            n_buf.at[turn, group],
            x_buf.at[turn, half_count + place],
            a_send.at[turn, group],
            a_recv.at[turn, place],
            "tm",
            half * half_count + peer,
        )

    def rows_later(group, turn, peer):
        return remote(
            n_buf.at[turn, group],
            x_buf.at[turn, place],
            l_send.at[turn, group],
            l_recv.at[turn, place],
            "tm",
            half_count + peer,
        )

    def rows_in(turn, sender):
        return remote(
            n_buf.at[turn, 0],
            x_buf.at[turn, half_count + sender],
            a_send.at[turn, 0],
            a_recv.at[turn, sender],
            "tm",
            half * half_count + sender,
        )

    def earlier_in(turn, sender):
        return remote(
            n_buf.at[turn, 0],
            x_buf.at[turn, sender],
            l_send.at[turn, 0],
            l_recv.at[turn, sender],
            "tm",
            sender,
        )

    def rows_home(turn):
        return pltpu.make_async_copy(
            n_buf.at[turn, place], x_buf.at[turn, half_count + place], self_sem.at[turn]
        )

    def merge(c):
        turn, first = chunk_groups(c)
        loop(1, chips, lambda step: partial_out(c, step).wait_recv())
        logs = [ll_buf[pl.ds(first, per_chunk), turn].reshape(rows, HEAD_DIM)]
        for step in range(1, chips):
            extra = pr_buf[step - 1, c, :, channels : channels + EXTRA].astype(F32)
            once = pltpu.roll(extra, EXTRA - SHARED_HEADS, 1)
            twice = pltpu.roll(extra, EXTRA - 2 * SHARED_HEADS, 1)
            logs.append(extra + (once + twice))
        top = functools.reduce(jnp.maximum, logs)
        shares = [jnp.exp2(log - top) for log in logs]
        total = functools.reduce(jnp.add, shares)
        shares = [share / total for share in shares]
        attended = []
        for h in all_heads:
            value = shares[0][:, h : h + 1] * ol_buf[
                pl.ds(first, per_chunk), turn, :, lanes_of(h)
            ].reshape(rows, HEAD_DIM)
            for step in range(1, chips):
                value = value + shares[step][:, h : h + 1] * pr_buf[
                    step - 1, c, :, lanes_of(h)
                ].astype(F32)
            attended.append(value.astype(BF16).astype(F32))
        squares = functools.reduce(jnp.add, [a * a for a in attended])
        mean = jnp.sum(squares, axis=-1, keepdims=True) / channels
        scale = lax.rsqrt(mean + 1e-05)
        for h in all_heads:
            normed = attended[h] * scale * pre_ref[:, lanes_of(h)]
            n_buf[turn, pl.ds(first, per_chunk), :, lanes_of(h)] = normed.reshape(
                per_chunk, ROWS, HEAD_DIM
            ).astype(BF16)
        for index in range(per_chunk):
            peer = first + index

            @pl.when(half == 0)
            def _():
                rows_later(peer, turn, peer).start()

            @pl.when(peer != place)
            def _():
                rows_out(peer, turn, peer).start()

            @pl.when(peer == place)
            def _():
                rows_home(turn).start()

    def result_out(turn, step):
        peer = lax.rem(place + step, half_count)
        return remote(
            o_buf.at[turn, peer],
            out_ref.at[place, turn],
            o_send.at[turn, step],
            o_recv.at[turn, step],
            "tm",
            half * half_count + peer,
        )

    def result_in(turn, step):
        sender = lax.rem(place - step + half_count, half_count)
        return remote(
            o_buf.at[turn, sender],
            out_ref.at[sender, turn],
            o_send.at[turn, step],
            o_recv.at[turn, step],
            "tm",
            half * half_count + sender,
        )

    def result_home(turn):
        return pltpu.make_async_copy(
            o_buf.at[turn, place], out_ref.at[place, turn], home_sem.at[turn]
        )

    def mix(turn):
        def take(step):
            rows_in(turn, lax.rem(place - step + half_count, half_count)).wait_recv()

        loop(1, half_count, take)
        rows_home(turn).wait()

        @pl.when(half == 1)
        def _():
            loop(0, half_count, lambda sender: earlier_in(turn, sender).wait_recv())

        values = x_buf[turn].reshape(both_rows, channels)
        across = (((1,), (1,)), ((), ()))
        b_in = lax.dot_general(values, w_in_ref[...], across, preferred_element_type=F32)
        c_out = lax.dot_general(
            values[own_rows:], w_out_ref[...], across, preferred_element_type=F32
        )
        gram = lax.dot_general(c_out, b_in, across, precision=HIGH, preferred_element_type=F32)
        mixing = [(gram * d_buf[turn, h]).astype(BF16) for h in all_heads]
        mixed = [
            jnp.dot(m, values[:, lanes_of(h)], preferred_element_type=F32)
            for m, h in zip(mixing, all_heads)
        ]
        mixed = [
            m + skips_ref[h] * values[own_rows:, lanes_of(h)].astype(F32)
            for m, h in zip(mixed, all_heads)
        ]
        squares = functools.reduce(jnp.add, [m * m for m in mixed])
        mean = jnp.sum(squares, axis=-1, keepdims=True) / channels
        scale = lax.rsqrt(mean + 1e-05)
        for h in all_heads:
            result = mixed[h] * scale * post_ref[:, lanes_of(h)]
            o_buf[turn, :, :, lanes_of(h)] = result.reshape(half_count, ROWS, HEAD_DIM).astype(BF16)
        loop(1, half_count, lambda step: result_out(turn, half_count - step).start())
        result_home(turn).start()

    def turn_of_loop(i):
        @pl.when(i < chunks)
        def _():
            attend_for(i, 1, True)
            loop(2, chips, lambda step: attend_for(i, step, False))

        @pl.when(i + ahead < chunks)
        def _():
            send_query(i + ahead)

        @pl.when((i >= lag_merge) & (i < chunks + lag_merge))
        def _():
            merge(i - lag_merge)

        @pl.when(i == 1)
        def _():
            send_steps()

        @pl.when(i == lag_mix - 1)
        def _():
            make_decays()

        c = i - lag_mix
        turn, first = chunk_groups(jnp.maximum(c, 0))

        @pl.when((c >= 0) & (c < chunks) & (place >= first) & (place < first + per_chunk))
        def _():
            mix(turn)

    loop(0, chunks + max(LAG_MIX), turn_of_loop)

    for part in range(KV_PARTS):
        for which in range(2):
            partner_kv(which, part).wait_send()
    for which in range(2):
        target = which * half_count + tm // 2

        @pl.when(target != tm)
        def _():
            step_copy(which, target, tm % 2).wait_send()

    def sent_chunk(c):
        def sent(step):
            query_out(c, step).wait_send()
            partial_out(c, step).wait_send()

        loop(1, chips, sent)

    loop(0, chunks, sent_chunk)

    for turn in range(turns):

        def sent_rows(group):
            @pl.when(half == 0)
            def _():
                rows_later(group, turn, group).wait_send()

            @pl.when(group != place)
            def _():
                rows_out(group, turn, group).wait_send()

        loop(0, half_count, sent_rows)

    for turn in range(turns):

        def finish(step):
            result_out(turn, step).wait_send()
            result_in(turn, step).wait_recv()

        loop(1, half_count, finish)
        result_home(turn).wait()


def body(
    queries,
    key_vectors,
    value_vectors,
    block_lists,
    step_sizes,
    decay_rates,
    skip_gains,
    pre_gain,
    state_in_weight,
    state_out_weight,
    post_gain,
):
    tokens, channels = queries.shape[1], queries.shape[2]
    space_count = lax.axis_size("space")
    tm_count = lax.axis_size("tm")
    half_count = tm_count // 2
    turns = tokens // (half_count * ROWS)
    chips = space_count // 2
    chunks = half_count * turns // PER_CHUNK
    rows = PER_CHUNK * ROWS
    state = state_in_weight.shape[1]
    hbm = pl.BlockSpec(memory_space=pl.ANY)
    dma = pltpu.SemaphoreType.DMA
    out = pl.pallas_call(
        functools.partial(kernel, (space_count, tm_count, block_lists.shape[1])),
        out_shape=jax.ShapeDtypeStruct((half_count, turns, ROWS, channels), BF16),
        in_specs=[hbm] * 11,
        out_specs=hbm,
        scratch_shapes=[
            pltpu.SMEM(block_lists.shape, jnp.int32),
            pltpu.SMEM(decay_rates.shape, F32),
            pltpu.SMEM(skip_gains.shape, F32),
            pltpu.VMEM((half_count, turns, ROWS, channels), BF16),
            pltpu.VMEM((tm_count, 2, tokens // tm_count, SHARED_HEADS), F32),
            pltpu.VMEM((1, channels), F32),
            pltpu.VMEM((state, channels), BF16),
            pltpu.VMEM((state, channels), BF16),
            pltpu.VMEM((1, channels), F32),
            pltpu.VMEM((2, 2, tokens, channels), BF16),
            pltpu.VMEM((chips - 1, chunks, PER_CHUNK, ROWS, channels), BF16),
            pltpu.VMEM((chips - 1, chunks, rows, channels + EXTRA), BF16),
            pltpu.VMEM((chips - 1, chunks, rows, channels + EXTRA), BF16),
            pltpu.VMEM((half_count, turns, ROWS, channels), F32),
            pltpu.VMEM((half_count, turns, ROWS, HEAD_DIM), F32),
            pltpu.VMEM((turns, half_count, ROWS, channels), BF16),
            pltpu.VMEM((turns, tm_count, ROWS, channels), BF16),
            pltpu.VMEM((turns, half_count, ROWS, channels), BF16),
            pltpu.VMEM((turns, SHARED_HEADS, half_count * ROWS, tm_count * ROWS), F32),
            dma((8,)),
            dma((2, KV_PARTS)),
            dma((2, KV_PARTS)),
            dma((2, KV_PARTS)),
            dma((2,)),
            dma((2,)),
            dma((2,)),
            dma((chips - 1, chunks)),
            dma((chips - 1, chunks)),
            dma((chips - 1, chunks)),
            dma((chips - 1, chunks)),
            dma((turns, half_count)),
            dma((turns, half_count)),
            dma((turns, half_count)),
            dma((turns, half_count)),
            dma((turns, half_count)),
            dma((turns, half_count)),
            dma((turns,)),
            dma((turns,)),
            pltpu.SemaphoreType.REGULAR,
        ],
        compiler_params=pltpu.CompilerParams(
            collective_id=0, has_side_effects=True, vmem_limit_bytes=VMEM_BYTES
        ),
        name="attend_and_mix",
    )(
        *(
            pltpu.with_memory_space_constraint(operand, pltpu.HBM)
            for operand in (
                block_lists,
                decay_rates,
                skip_gains,
                queries.reshape(half_count, turns, ROWS, channels),
                key_vectors.reshape(tokens, channels),
                value_vectors.reshape(tokens, channels),
                step_sizes,
                pre_gain.reshape(1, channels),
                state_in_weight.T,
                state_out_weight.T,
                post_gain.reshape(1, channels),
            )
        )
    )
    return out.reshape(1, tokens, channels)


def solution(mesh):
    placed = (
        P("tm", "space", None),
        P("tm", "space", None),
        P("tm", "space", None),
        P(),
        P(None, ("space", "tm"), None),
        P(),
        P(),
        P(),
        P(),
        P(),
        P(),
    )
    return jax.shard_map(
        body, mesh=mesh, in_specs=placed, out_specs=P("tm", "space", None), check_vma=False
    )
```

```python
import functools
import math

import jax
import jax.numpy as jnp
from jax import lax
from jax.experimental import pallas as pl
from jax.experimental.pallas import tpu as pltpu
from jax.sharding import PartitionSpec as P

SHARED_HEADS = 16
HEAD_DIM = 128
ROWS = 8
PER_CHUNK = 1
AHEAD = (5, 5)
LAG_MERGE = (4, 3)
LAG_MIX = (8, 7)
KV_PARTS = 1
EXTRA = 128
VMEM_BYTES = 44 * 1024 * 1024
MESH = pl.DeviceIdType.MESH
F32 = jnp.float32
BF16 = jnp.bfloat16
HIGH = lax.Precision.HIGHEST


def remote(src, dst, send_sem, recv_sem, axis, index):
    return pltpu.make_async_remote_copy(
        src_ref=src,
        dst_ref=dst,
        send_sem=send_sem,
        recv_sem=recv_sem,
        device_id={axis: index},
        device_id_type=MESH,
    )


def loop(low, high, act):
    if high - low == 1:
        act(low)
    elif high > low:

        def turn(i, carry):
            act(i)
            return carry

        lax.fori_loop(low, high, turn, 0)


def lanes_of(head):
    return slice(head * HEAD_DIM, (head + 1) * HEAD_DIM)


def attend(query, key, value, bias, heads):
    factor = math.log2(math.e) / math.sqrt(HEAD_DIM)
    across = (((1,), (1,)), ((), ()))
    scores = [
        lax.dot_general(query(h), key(h), across, preferred_element_type=F32) * factor + bias
        for h in heads
    ]
    tops = [jnp.max(s, axis=-1, keepdims=True) for s in scores]
    weights = [jnp.exp2(s - m) for s, m in zip(scores, tops)]
    totals = [jnp.sum(w, axis=-1, keepdims=True) for w in weights]
    sums = [
        jnp.dot(w.astype(BF16), value(h), preferred_element_type=F32) for w, h in zip(weights, heads)
    ]
    return [s / t for s, t in zip(sums, totals)], tops, totals


def packed(columns, heads, lane, into):
    for h, column in zip(heads, columns):
        into = jnp.where(lane == h, column, into)
    return into


def kernel(
    dims,
    lists_hbm,
    rates_hbm,
    skips_hbm,
    q_hbm,
    k_hbm,
    v_hbm,
    steps_hbm,
    pre_hbm,
    w_in_hbm,
    w_out_hbm,
    post_hbm,
    out_ref,
    lists_ref,
    rates_ref,
    skips_ref,
    q_ref,
    steps_ref,
    pre_ref,
    w_in_ref,
    w_out_ref,
    post_ref,
    kv_buf,
    qr_buf,
    ps_buf,
    pr_buf,
    ol_buf,
    ll_buf,
    n_buf,
    x_buf,
    o_buf,
    d_buf,
    load_sem,
    own_sem,
    kv_send,
    kv_recv,
    step_send,
    step_recv,
    step_own,
    q_send,
    q_recv,
    p_send,
    p_recv,
    a_send,
    a_recv,
    l_send,
    l_recv,
    o_send,
    o_recv,
    self_sem,
    home_sem,
    ready_sem,
):
    space_count, tm_count, list_width = dims
    half_count, turns, _, channels = q_hbm.shape
    tokens = half_count * turns * ROWS
    per_chunk = PER_CHUNK
    sets = half_count // per_chunk
    chunks = sets * turns
    rows = per_chunk * ROWS
    chips = space_count // 2
    all_heads = range(SHARED_HEADS)
    space = lax.axis_index("space")
    tm = lax.axis_index("tm")
    half = tm // half_count
    place = tm % half_count
    chip = space // 2
    core = space % 2
    partner = chip * 2 + 1 - core
    ahead, lag_merge, lag_mix = (
        pair[1] + (1 - core) * (pair[0] - pair[1]) for pair in (AHEAD, LAG_MERGE, LAG_MIX)
    )

    barrier = pltpu.get_barrier_semaphore()

    def greet_chip(step):
        peer = lax.rem(chip + step, chips) * 2 + 1 - core
        pl.semaphore_signal(barrier, inc=1, device_id={"space": peer}, device_id_type=MESH)

    def greet_frame(peer):
        pl.semaphore_signal(barrier, inc=1, device_id={"tm": peer}, device_id_type=MESH)

    def answer_frame(peer):
        pl.semaphore_signal(ready_sem, inc=1, device_id={"tm": peer}, device_id_type=MESH)

    loop(1, chips, greet_chip)
    pl.semaphore_signal(barrier, inc=1, device_id={"space": partner}, device_id_type=MESH)
    lax.fori_loop(tm + 1, tm_count, lambda peer, carry: (greet_frame(peer), carry)[1], 0)

    part_width = channels // KV_PARTS

    def kv_span(part):
        return pl.ds(part * part_width, part_width)

    def own_kv(which, part):
        source = (k_hbm, v_hbm)[which]
        return pltpu.make_async_copy(
            source.at[:, kv_span(part)],
            kv_buf.at[which, core, :, kv_span(part)],
            own_sem.at[which, part],
        )

    def partner_kv(which, part):
        source = (k_hbm, v_hbm)[which]
        return remote(
            source.at[:, kv_span(part)],
            kv_buf.at[which, core, :, kv_span(part)],
            kv_send.at[which, part],
            kv_recv.at[which, part],
            "space",
            partner,
        )

    load_q = pltpu.make_async_copy(q_hbm, q_ref, load_sem.at[0])
    load_q.start()
    for part in range(KV_PARTS):
        for which in range(2):
            own_kv(which, part).start()
    loads = [
        pltpu.make_async_copy(source, target, load_sem.at[1 + index])
        for index, (source, target) in enumerate(
            (
                (lists_hbm, lists_ref),
                (rates_hbm, rates_ref),
                (skips_hbm, skips_ref),
                (pre_hbm, pre_ref),
                (w_in_hbm, w_in_ref),
                (w_out_hbm, w_out_ref),
                (post_hbm, post_ref),
            )
        )
    ]
    for load in loads:
        load.start()

    def chunk_groups(c):
        return c // sets, (sets - 1 - c % sets) * per_chunk

    def query_out(c, step):
        turn, first = chunk_groups(c)
        return remote(
            q_hbm.at[pl.ds(first, per_chunk), turn],
            qr_buf.at[step - 1, c],
            q_send.at[step - 1, c],
            q_recv.at[step - 1, c],
            "space",
            lax.rem(chip + step, chips) * 2 + 1 - core,
        )

    def partial_out(c, step):
        return remote(
            ps_buf.at[step - 1, c],
            pr_buf.at[step - 1, c],
            p_send.at[step - 1, c],
            p_recv.at[step - 1, c],
            "space",
            lax.rem(chip - step + chips, chips) * 2 + 1 - core,
        )

    def send_query(c):
        loop(1, chips, lambda step: query_out(c, step).start())

    pl.semaphore_wait(barrier, chips + tm)

    send_query(0)
    for part in range(KV_PARTS):
        for which in range(2):
            partner_kv(which, part).start()
    lax.fori_loop(1, jnp.minimum(ahead, chunks), lambda c, carry: (send_query(c), carry)[1], 0)
    lax.fori_loop(0, tm, lambda peer, carry: (answer_frame(peer), carry)[1], 0)

    def step_copy(which, target, part):
        return remote(
            steps_hbm,
            steps_ref.at[:, part],
            step_send.at[which],
            step_recv.at[part],
            "tm",
            target,
        )

    def step_local(part):
        return pltpu.make_async_copy(steps_hbm, steps_ref.at[:, part], step_own.at[part])

    for load in loads:
        load.wait()
    load_q.wait()

    def key_of(h):
        return kv_buf[0, :, :, lanes_of(h)].reshape(2 * tokens, HEAD_DIM)

    def value_of(h):
        return kv_buf[1, :, :, lanes_of(h)].reshape(2 * tokens, HEAD_DIM)

    block_of = chip * 2 + lax.broadcasted_iota(jnp.int32, (1, 2 * tokens), 1) // tokens

    def bias_of(owner):
        chosen = block_of == lists_ref[owner, 0]
        for entry in range(1, list_width):
            chosen = chosen | (block_of == lists_ref[owner, entry])
        return jnp.where(chosen, 0.0, -1e30).astype(F32)

    own_rows = half_count * ROWS
    both_rows = tm_count * ROWS

    def send_steps():
        @pl.when(tm < tm_count - 1)
        def _():
            pl.semaphore_wait(ready_sem, tm_count - 1 - tm)

        for which in range(2):
            target = which * half_count + tm // 2
            part = tm % 2

            @pl.when(target != tm)
            def _():
                step_copy(which, target, part).start()

            @pl.when(target == tm)
            def _():
                step_local(part).start()

    def make_decays():
        for part in range(2):
            origin = 2 * place + part

            @pl.when(origin != tm)
            def _():
                step_copy(0, origin, part).wait_recv()

            @pl.when(origin == tm)
            def _():
                step_local(part).wait()

        steps = steps_ref[...].reshape(tm_count, turns, ROWS, SHARED_HEADS)
        earlier, later = steps[:half_count], steps[half_count:]
        own = jnp.where(half == 1, later, earlier)
        steps = jnp.concatenate([earlier, own], axis=0)
        counted = jnp.concatenate([jnp.where(half == 1, earlier, 0.0), own], axis=0)
        run = [counted[0]]
        for frame in range(1, tm_count):
            run.append(run[-1] + counted[frame])
        run = jnp.stack(run)
        row = half_count * ROWS + lax.broadcasted_iota(jnp.int32, (own_rows, both_rows), 0)
        col = lax.broadcasted_iota(jnp.int32, (own_rows, both_rows), 1)
        counts = (row % ROWS == col % ROWS) & (col // ROWS <= row // ROWS)
        counts = counts & (col >= (1 - half) * own_rows)
        for turn in range(turns):
            total = run[:, turn].reshape(both_rows, SHARED_HEADS)
            total_t = jnp.transpose(total)
            steps_t = jnp.transpose(steps[:, turn].reshape(both_rows, SHARED_HEADS))
            for head in all_heads:
                gap = total_t[head : head + 1, :] - total[own_rows:, head : head + 1]
                decay = jnp.exp(jnp.where(counts, gap * rates_ref[head], -1e30))
                d_buf[turn, head] = decay * steps_t[head : head + 1, :]

    for part in range(KV_PARTS):
        for which in range(2):
            own_kv(which, part).wait()
            partner_kv(which, part).wait_recv()

    @pl.when(half == 0)
    def _():
        x_buf[:, 0:half_count] = jnp.zeros((turns, half_count, ROWS, channels), BF16)

    chunk_lane = lax.broadcasted_iota(jnp.int32, (rows, HEAD_DIM), 1)

    def attend_for(c, step, with_own):
        turn, first = chunk_groups(c)
        query_out(c, step).wait_recv()
        owner = lax.rem(chip - step + chips, chips) * 2 + 1 - core
        query = qr_buf[step - 1, c].reshape(rows, channels)
        bias = bias_of(owner)
        skip = rows if with_own else 0
        if with_own:
            mine = q_ref[pl.ds(first, per_chunk), turn].reshape(rows, channels)
            query = jnp.concatenate([mine.astype(F32), query.astype(F32)], axis=0).astype(BF16)
            row_of = lax.broadcasted_iota(jnp.int32, (2 * rows, 2 * tokens), 0)
            bias = jnp.where(row_of < rows, bias_of(space), bias)
        summed, top, total = attend(
            lambda h: query[:, lanes_of(h)], key_of, value_of, bias, all_heads
        )
        slot_of = lax.broadcasted_iota(jnp.int32, (skip + rows, HEAD_DIM), 1) % SHARED_HEADS
        for h, values in zip(all_heads, summed):
            ps_buf[step - 1, c, :, lanes_of(h)] = values[skip:].astype(BF16)
        tops = packed(top, all_heads, slot_of, jnp.zeros((skip + rows, HEAD_DIM), F32))
        totals = packed(total, all_heads, slot_of, jnp.ones((skip + rows, HEAD_DIM), F32))
        both_logs = tops + jnp.log2(totals)
        logs = both_logs[skip:]
        big = logs.astype(BF16)
        rest = logs - big.astype(F32)
        middle = rest.astype(BF16)
        small = (rest - middle.astype(F32)).astype(BF16)
        extra = jnp.where(
            chunk_lane < SHARED_HEADS,
            big.astype(F32),
            jnp.where(chunk_lane < 2 * SHARED_HEADS, middle.astype(F32), small.astype(F32)),
        )
        ps_buf[step - 1, c, :, channels : channels + EXTRA] = extra.astype(BF16)
        partial_out(c, step).start()
        if with_own:
            for h, values in zip(all_heads, summed):
                ol_buf[pl.ds(first, per_chunk), turn, :, lanes_of(h)] = values[:skip].reshape(
                    per_chunk, ROWS, HEAD_DIM
                )
            ll_buf[pl.ds(first, per_chunk), turn] = both_logs[:skip].reshape(
                per_chunk, ROWS, HEAD_DIM
            )

    def rows_out(group, turn, peer):
        return remote(
            n_buf.at[turn, group],
            x_buf.at[turn, half_count + place],
            a_send.at[turn, group],
            a_recv.at[turn, place],
            "tm",
            half * half_count + peer,
        )

    def rows_later(group, turn, peer):
        return remote(
            n_buf.at[turn, group],
            x_buf.at[turn, place],
            l_send.at[turn, group],
            l_recv.at[turn, place],
            "tm",
            half_count + peer,
        )

    def rows_in(turn, sender):
        return remote(
            n_buf.at[turn, 0],
            x_buf.at[turn, half_count + sender],
            a_send.at[turn, 0],
            a_recv.at[turn, sender],
            "tm",
            half * half_count + sender,
        )

    def earlier_in(turn, sender):
        return remote(
            n_buf.at[turn, 0],
            x_buf.at[turn, sender],
            l_send.at[turn, 0],
            l_recv.at[turn, sender],
            "tm",
            sender,
        )

    def rows_home(turn):
        return pltpu.make_async_copy(
            n_buf.at[turn, place], x_buf.at[turn, half_count + place], self_sem.at[turn]
        )

    def merge(c):
        turn, first = chunk_groups(c)
        loop(1, chips, lambda step: partial_out(c, step).wait_recv())
        logs = [ll_buf[pl.ds(first, per_chunk), turn].reshape(rows, HEAD_DIM)]
        for step in range(1, chips):
            extra = pr_buf[step - 1, c, :, channels : channels + EXTRA].astype(F32)
            once = pltpu.roll(extra, EXTRA - SHARED_HEADS, 1)
            twice = pltpu.roll(extra, EXTRA - 2 * SHARED_HEADS, 1)
            logs.append(extra + (once + twice))
        top = functools.reduce(jnp.maximum, logs)
        shares = [jnp.exp2(log - top) for log in logs]
        total = functools.reduce(jnp.add, shares)
        shares = [share / total for share in shares]
        attended = []
        for h in all_heads:
            value = shares[0][:, h : h + 1] * ol_buf[
                pl.ds(first, per_chunk), turn, :, lanes_of(h)
            ].reshape(rows, HEAD_DIM)
            for step in range(1, chips):
                value = value + shares[step][:, h : h + 1] * pr_buf[
                    step - 1, c, :, lanes_of(h)
                ].astype(F32)
            attended.append(value.astype(BF16).astype(F32))
        squares = functools.reduce(jnp.add, [a * a for a in attended])
        mean = jnp.sum(squares, axis=-1, keepdims=True) / channels
        scale = lax.rsqrt(mean + 1e-05)
        for h in all_heads:
            normed = attended[h] * scale * pre_ref[:, lanes_of(h)]
            n_buf[turn, pl.ds(first, per_chunk), :, lanes_of(h)] = normed.reshape(
                per_chunk, ROWS, HEAD_DIM
            ).astype(BF16)
        for index in range(per_chunk):
            peer = first + index

            @pl.when(half == 0)
            def _():
                rows_later(peer, turn, peer).start()

            @pl.when(peer != place)
            def _():
                rows_out(peer, turn, peer).start()

            @pl.when(peer == place)
            def _():
                rows_home(turn).start()

    def result_out(turn, step):
        peer = lax.rem(place + step, half_count)
        return remote(
            o_buf.at[turn, peer],
            out_ref.at[place, turn],
            o_send.at[turn, step],
            o_recv.at[turn, step],
            "tm",
            half * half_count + peer,
        )

    def result_in(turn, step):
        sender = lax.rem(place - step + half_count, half_count)
        return remote(
            o_buf.at[turn, sender],
            out_ref.at[sender, turn],
            o_send.at[turn, step],
            o_recv.at[turn, step],
            "tm",
            half * half_count + sender,
        )

    def result_home(turn):
        return pltpu.make_async_copy(
            o_buf.at[turn, place], out_ref.at[place, turn], home_sem.at[turn]
        )

    def mix(turn):
        def take(step):
            rows_in(turn, lax.rem(place - step + half_count, half_count)).wait_recv()

        loop(1, half_count, take)
        rows_home(turn).wait()

        @pl.when(half == 1)
        def _():
            loop(0, half_count, lambda sender: earlier_in(turn, sender).wait_recv())

        values = x_buf[turn].reshape(both_rows, channels)
        across = (((1,), (1,)), ((), ()))
        b_in = lax.dot_general(values, w_in_ref[...], across, preferred_element_type=F32)
        c_out = lax.dot_general(
            values[own_rows:], w_out_ref[...], across, preferred_element_type=F32
        )
        gram = lax.dot_general(c_out, b_in, across, precision=HIGH, preferred_element_type=F32)
        mixing = [(gram * d_buf[turn, h]).astype(BF16) for h in all_heads]
        mixed = [
            jnp.dot(m, values[:, lanes_of(h)], preferred_element_type=F32)
            for m, h in zip(mixing, all_heads)
        ]
        mixed = [
            m + skips_ref[h] * values[own_rows:, lanes_of(h)].astype(F32)
            for m, h in zip(mixed, all_heads)
        ]
        squares = functools.reduce(jnp.add, [m * m for m in mixed])
        mean = jnp.sum(squares, axis=-1, keepdims=True) / channels
        scale = lax.rsqrt(mean + 1e-05)
        for h in all_heads:
            result = mixed[h] * scale * post_ref[:, lanes_of(h)]
            o_buf[turn, :, :, lanes_of(h)] = result.reshape(half_count, ROWS, HEAD_DIM).astype(BF16)
        loop(1, half_count, lambda step: result_out(turn, half_count - step).start())
        result_home(turn).start()

    def turn_of_loop(i):
        @pl.when(i < chunks)
        def _():
            attend_for(i, 1, True)
            loop(2, chips, lambda step: attend_for(i, step, False))

        @pl.when(i + ahead < chunks)
        def _():
            send_query(i + ahead)

        @pl.when((i >= lag_merge) & (i < chunks + lag_merge))
        def _():
            merge(i - lag_merge)

        @pl.when(i == 1)
        def _():
            send_steps()

        @pl.when(i == lag_mix - 1)
        def _():
            make_decays()

        c = i - lag_mix
        turn, first = chunk_groups(jnp.maximum(c, 0))

        @pl.when((c >= 0) & (c < chunks) & (place >= first) & (place < first + per_chunk))
        def _():
            mix(turn)

    loop(0, chunks + max(LAG_MIX), turn_of_loop)

    for part in range(KV_PARTS):
        for which in range(2):
            partner_kv(which, part).wait_send()
    for which in range(2):
        target = which * half_count + tm // 2

        @pl.when(target != tm)
        def _():
            step_copy(which, target, tm % 2).wait_send()

    def sent_chunk(c):
        def sent(step):
            query_out(c, step).wait_send()
            partial_out(c, step).wait_send()

        loop(1, chips, sent)

    loop(0, chunks, sent_chunk)

    for turn in range(turns):

        def sent_rows(group):
            @pl.when(half == 0)
            def _():
                rows_later(group, turn, group).wait_send()

            @pl.when(group != place)
            def _():
                rows_out(group, turn, group).wait_send()

        loop(0, half_count, sent_rows)

    for turn in range(turns):

        def finish(step):
            result_out(turn, step).wait_send()
            result_in(turn, step).wait_recv()

        loop(1, half_count, finish)
        result_home(turn).wait()


def body(
    queries,
    key_vectors,
    value_vectors,
    block_lists,
    step_sizes,
    decay_rates,
    skip_gains,
    pre_gain,
    state_in_weight,
    state_out_weight,
    post_gain,
):
    tokens, channels = queries.shape[1], queries.shape[2]
    space_count = lax.axis_size("space")
    tm_count = lax.axis_size("tm")
    half_count = tm_count // 2
    turns = tokens // (half_count * ROWS)
    chips = space_count // 2
    chunks = half_count * turns // PER_CHUNK
    rows = PER_CHUNK * ROWS
    state = state_in_weight.shape[1]
    hbm = pl.BlockSpec(memory_space=pl.ANY)
    dma = pltpu.SemaphoreType.DMA
    out = pl.pallas_call(
        functools.partial(kernel, (space_count, tm_count, block_lists.shape[1])),
        out_shape=jax.ShapeDtypeStruct((half_count, turns, ROWS, channels), BF16),
        in_specs=[hbm] * 11,
        out_specs=hbm,
        scratch_shapes=[
            pltpu.SMEM(block_lists.shape, jnp.int32),
            pltpu.SMEM(decay_rates.shape, F32),
            pltpu.SMEM(skip_gains.shape, F32),
            pltpu.VMEM((half_count, turns, ROWS, channels), BF16),
            pltpu.VMEM((tm_count, 2, tokens // tm_count, SHARED_HEADS), F32),
            pltpu.VMEM((1, channels), F32),
            pltpu.VMEM((state, channels), BF16),
            pltpu.VMEM((state, channels), BF16),
            pltpu.VMEM((1, channels), F32),
            pltpu.VMEM((2, 2, tokens, channels), BF16),
            pltpu.VMEM((chips - 1, chunks, PER_CHUNK, ROWS, channels), BF16),
            pltpu.VMEM((chips - 1, chunks, rows, channels + EXTRA), BF16),
            pltpu.VMEM((chips - 1, chunks, rows, channels + EXTRA), BF16),
            pltpu.VMEM((half_count, turns, ROWS, channels), F32),
            pltpu.VMEM((half_count, turns, ROWS, HEAD_DIM), F32),
            pltpu.VMEM((turns, half_count, ROWS, channels), BF16),
            pltpu.VMEM((turns, tm_count, ROWS, channels), BF16),
            pltpu.VMEM((turns, half_count, ROWS, channels), BF16),
            pltpu.VMEM((turns, SHARED_HEADS, half_count * ROWS, tm_count * ROWS), F32),
            dma((8,)),
            dma((2, KV_PARTS)),
            dma((2, KV_PARTS)),
            dma((2, KV_PARTS)),
            dma((2,)),
            dma((2,)),
            dma((2,)),
            dma((chips - 1, chunks)),
            dma((chips - 1, chunks)),
            dma((chips - 1, chunks)),
            dma((chips - 1, chunks)),
            dma((turns, half_count)),
            dma((turns, half_count)),
            dma((turns, half_count)),
            dma((turns, half_count)),
            dma((turns, half_count)),
            dma((turns, half_count)),
            dma((turns,)),
            dma((turns,)),
            pltpu.SemaphoreType.REGULAR,
        ],
        compiler_params=pltpu.CompilerParams(
            collective_id=0, has_side_effects=True, vmem_limit_bytes=VMEM_BYTES
        ),
        name="attend_and_mix",
    )(
        *(
            pltpu.with_memory_space_constraint(operand, pltpu.HBM)
            for operand in (
                block_lists,
                decay_rates,
                skip_gains,
                queries.reshape(half_count, turns, ROWS, channels),
                key_vectors.reshape(tokens, channels),
                value_vectors.reshape(tokens, channels),
                step_sizes,
                pre_gain.reshape(1, channels),
                state_in_weight.T,
                state_out_weight.T,
                post_gain.reshape(1, channels),
            )
        )
    )
    return out.reshape(1, tokens, channels)


def solution(mesh):
    placed = (
        P("tm", "space", None),
        P("tm", "space", None),
        P("tm", "space", None),
        P(),
        P(None, ("space", "tm"), None),
        P(),
        P(),
        P(),
        P(),
        P(),
        P(),
    )
    return jax.shard_map(
        body, mesh=mesh, in_specs=placed, out_specs=P("tm", "space", None), check_vma=False
    )
```

```python
import functools
import math

import jax
import jax.numpy as jnp
from jax import lax
from jax.experimental import pallas as pl
from jax.experimental.pallas import tpu as pltpu
from jax.sharding import PartitionSpec as P

SHARED_HEADS = 16
HEAD_DIM = 128
ROWS = 8
PER_CHUNK = 1
AHEAD = (5, 5)
LAG_MERGE = (4, 3)
LAG_MIX = (8, 7)
KV_PARTS = 1
EXTRA = 128
VMEM_BYTES = 44 * 1024 * 1024
MESH = pl.DeviceIdType.MESH
F32 = jnp.float32
BF16 = jnp.bfloat16
HIGH = lax.Precision.HIGHEST


def remote(src, dst, send_sem, recv_sem, axis, index):
    return pltpu.make_async_remote_copy(
        src_ref=src,
        dst_ref=dst,
        send_sem=send_sem,
        recv_sem=recv_sem,
        device_id={axis: index},
        device_id_type=MESH,
    )


def loop(low, high, act):
    if high - low == 1:
        act(low)
    elif high > low:

        def turn(i, carry):
            act(i)
            return carry

        lax.fori_loop(low, high, turn, 0)


def lanes_of(head):
    return slice(head * HEAD_DIM, (head + 1) * HEAD_DIM)


def attend(query, key, value, bias, heads):
    factor = math.log2(math.e) / math.sqrt(HEAD_DIM)
    across = (((1,), (1,)), ((), ()))
    scores = [
        lax.dot_general(query(h), key(h), across, preferred_element_type=F32) * factor + bias
        for h in heads
    ]
    tops = [jnp.max(s, axis=-1, keepdims=True) for s in scores]
    weights = [jnp.exp2(s - m) for s, m in zip(scores, tops)]
    totals = [jnp.sum(w, axis=-1, keepdims=True) for w in weights]
    sums = [
        jnp.dot(w.astype(BF16), value(h), preferred_element_type=F32) for w, h in zip(weights, heads)
    ]
    return [s / t for s, t in zip(sums, totals)], tops, totals


def packed(columns, heads, lane, into):
    for h, column in zip(heads, columns):
        into = jnp.where(lane == h, column, into)
    return into


def kernel(
    dims,
    lists_hbm,
    rates_hbm,
    skips_hbm,
    q_hbm,
    k_hbm,
    v_hbm,
    steps_hbm,
    pre_hbm,
    w_in_hbm,
    w_out_hbm,
    post_hbm,
    out_ref,
    lists_ref,
    rates_ref,
    skips_ref,
    q_ref,
    steps_ref,
    pre_ref,
    w_in_ref,
    w_out_ref,
    post_ref,
    kv_buf,
    qr_buf,
    ps_buf,
    pr_buf,
    ol_buf,
    ll_buf,
    n_buf,
    x_buf,
    o_buf,
    d_buf,
    load_sem,
    own_sem,
    kv_send,
    kv_recv,
    step_send,
    step_recv,
    step_own,
    q_send,
    q_recv,
    p_send,
    p_recv,
    a_send,
    a_recv,
    l_send,
    l_recv,
    o_send,
    o_recv,
    self_sem,
    home_sem,
    ready_sem,
):
    space_count, tm_count, list_width = dims
    half_count, turns, _, channels = q_hbm.shape
    tokens = half_count * turns * ROWS
    per_chunk = PER_CHUNK
    sets = half_count // per_chunk
    chunks = sets * turns
    rows = per_chunk * ROWS
    chips = space_count // 2
    all_heads = range(SHARED_HEADS)
    space = lax.axis_index("space")
    tm = lax.axis_index("tm")
    half = tm // half_count
    place = tm % half_count
    chip = space // 2
    core = space % 2
    partner = chip * 2 + 1 - core
    ahead, lag_merge, lag_mix = (
        pair[1] + (1 - core) * (pair[0] - pair[1]) for pair in (AHEAD, LAG_MERGE, LAG_MIX)
    )

    barrier = pltpu.get_barrier_semaphore()

    def greet_chip(step):
        peer = lax.rem(chip + step, chips) * 2 + 1 - core
        pl.semaphore_signal(barrier, inc=1, device_id={"space": peer}, device_id_type=MESH)

    def greet_frame(peer):
        pl.semaphore_signal(barrier, inc=1, device_id={"tm": peer}, device_id_type=MESH)

    def answer_frame(peer):
        pl.semaphore_signal(ready_sem, inc=1, device_id={"tm": peer}, device_id_type=MESH)

    pl.semaphore_signal(barrier, inc=1, device_id={"space": partner}, device_id_type=MESH)
    loop(1, chips, greet_chip)
    lax.fori_loop(tm + 1, tm_count, lambda peer, carry: (greet_frame(peer), carry)[1], 0)

    part_width = channels // KV_PARTS

    def kv_span(part):
        return pl.ds(part * part_width, part_width)

    def own_kv(which, part):
        source = (k_hbm, v_hbm)[which]
        return pltpu.make_async_copy(
            source.at[:, kv_span(part)],
            kv_buf.at[which, core, :, kv_span(part)],
            own_sem.at[which, part],
        )

    def partner_kv(which, part):
        source = (k_hbm, v_hbm)[which]
        return remote(
            source.at[:, kv_span(part)],
            kv_buf.at[which, core, :, kv_span(part)],
            kv_send.at[which, part],
            kv_recv.at[which, part],
            "space",
            partner,
        )

    load_q = pltpu.make_async_copy(q_hbm, q_ref, load_sem.at[0])
    load_q.start()
    for part in range(KV_PARTS):
        for which in range(2):
            own_kv(which, part).start()
    loads = [
        pltpu.make_async_copy(source, target, load_sem.at[1 + index])
        for index, (source, target) in enumerate(
            (
                (lists_hbm, lists_ref),
                (rates_hbm, rates_ref),
                (skips_hbm, skips_ref),
                (pre_hbm, pre_ref),
                (w_in_hbm, w_in_ref),
                (w_out_hbm, w_out_ref),
                (post_hbm, post_ref),
            )
        )
    ]
    for load in loads:
        load.start()

    def chunk_groups(c):
        return c // sets, (sets - 1 - c % sets) * per_chunk

    def query_out(c, step):
        turn, first = chunk_groups(c)
        return remote(
            q_hbm.at[pl.ds(first, per_chunk), turn],
            qr_buf.at[step - 1, c],
            q_send.at[step - 1, c],
            q_recv.at[step - 1, c],
            "space",
            lax.rem(chip + step, chips) * 2 + 1 - core,
        )

    def partial_out(c, step):
        return remote(
            ps_buf.at[step - 1, c],
            pr_buf.at[step - 1, c],
            p_send.at[step - 1, c],
            p_recv.at[step - 1, c],
            "space",
            lax.rem(chip - step + chips, chips) * 2 + 1 - core,
        )

    def send_query(c):
        loop(1, chips, lambda step: query_out(c, step).start())

    pl.semaphore_wait(barrier, chips + tm)

    send_query(0)
    for part in range(KV_PARTS):
        for which in range(2):
            partner_kv(which, part).start()
    lax.fori_loop(1, jnp.minimum(ahead, chunks), lambda c, carry: (send_query(c), carry)[1], 0)
    lax.fori_loop(0, tm, lambda peer, carry: (answer_frame(peer), carry)[1], 0)

    def step_copy(which, target, part):
        return remote(
            steps_hbm,
            steps_ref.at[:, part],
            step_send.at[which],
            step_recv.at[part],
            "tm",
            target,
        )

    def step_local(part):
        return pltpu.make_async_copy(steps_hbm, steps_ref.at[:, part], step_own.at[part])

    for load in loads:
        load.wait()
    load_q.wait()

    def key_of(h):
        return kv_buf[0, :, :, lanes_of(h)].reshape(2 * tokens, HEAD_DIM)

    def value_of(h):
        return kv_buf[1, :, :, lanes_of(h)].reshape(2 * tokens, HEAD_DIM)

    block_of = chip * 2 + lax.broadcasted_iota(jnp.int32, (1, 2 * tokens), 1) // tokens

    def bias_of(owner):
        chosen = block_of == lists_ref[owner, 0]
        for entry in range(1, list_width):
            chosen = chosen | (block_of == lists_ref[owner, entry])
        return jnp.where(chosen, 0.0, -1e30).astype(F32)

    own_rows = half_count * ROWS
    both_rows = tm_count * ROWS

    def send_steps():
        @pl.when(tm < tm_count - 1)
        def _():
            pl.semaphore_wait(ready_sem, tm_count - 1 - tm)

        for which in range(2):
            target = which * half_count + tm // 2
            part = tm % 2

            @pl.when(target != tm)
            def _():
                step_copy(which, target, part).start()

            @pl.when(target == tm)
            def _():
                step_local(part).start()

    def make_decays():
        for part in range(2):
            origin = 2 * place + part

            @pl.when(origin != tm)
            def _():
                step_copy(0, origin, part).wait_recv()

            @pl.when(origin == tm)
            def _():
                step_local(part).wait()

        steps = steps_ref[...].reshape(tm_count, turns, ROWS, SHARED_HEADS)
        earlier, later = steps[:half_count], steps[half_count:]
        own = jnp.where(half == 1, later, earlier)
        steps = jnp.concatenate([earlier, own], axis=0)
        counted = jnp.concatenate([jnp.where(half == 1, earlier, 0.0), own], axis=0)
        run = [counted[0]]
        for frame in range(1, tm_count):
            run.append(run[-1] + counted[frame])
        run = jnp.stack(run)
        row = half_count * ROWS + lax.broadcasted_iota(jnp.int32, (own_rows, both_rows), 0)
        col = lax.broadcasted_iota(jnp.int32, (own_rows, both_rows), 1)
        counts = (row % ROWS == col % ROWS) & (col // ROWS <= row // ROWS)
        counts = counts & (col >= (1 - half) * own_rows)
        for turn in range(turns):
            total = run[:, turn].reshape(both_rows, SHARED_HEADS)
            total_t = jnp.transpose(total)
            steps_t = jnp.transpose(steps[:, turn].reshape(both_rows, SHARED_HEADS))
            for head in all_heads:
                gap = total_t[head : head + 1, :] - total[own_rows:, head : head + 1]
                decay = jnp.exp(jnp.where(counts, gap * rates_ref[head], -1e30))
                d_buf[turn, head] = decay * steps_t[head : head + 1, :]

    for part in range(KV_PARTS):
        for which in range(2):
            own_kv(which, part).wait()
            partner_kv(which, part).wait_recv()

    @pl.when(half == 0)
    def _():
        x_buf[:, 0:half_count] = jnp.zeros((turns, half_count, ROWS, channels), BF16)

    chunk_lane = lax.broadcasted_iota(jnp.int32, (rows, HEAD_DIM), 1)

    def attend_for(c, step, with_own):
        turn, first = chunk_groups(c)
        query_out(c, step).wait_recv()
        owner = lax.rem(chip - step + chips, chips) * 2 + 1 - core
        query = qr_buf[step - 1, c].reshape(rows, channels)
        bias = bias_of(owner)
        skip = rows if with_own else 0
        if with_own:
            mine = q_ref[pl.ds(first, per_chunk), turn].reshape(rows, channels)
            query = jnp.concatenate([mine.astype(F32), query.astype(F32)], axis=0).astype(BF16)
            row_of = lax.broadcasted_iota(jnp.int32, (2 * rows, 2 * tokens), 0)
            bias = jnp.where(row_of < rows, bias_of(space), bias)
        summed, top, total = attend(
            lambda h: query[:, lanes_of(h)], key_of, value_of, bias, all_heads
        )
        slot_of = lax.broadcasted_iota(jnp.int32, (skip + rows, HEAD_DIM), 1) % SHARED_HEADS
        for h, values in zip(all_heads, summed):
            ps_buf[step - 1, c, :, lanes_of(h)] = values[skip:].astype(BF16)
        tops = packed(top, all_heads, slot_of, jnp.zeros((skip + rows, HEAD_DIM), F32))
        totals = packed(total, all_heads, slot_of, jnp.ones((skip + rows, HEAD_DIM), F32))
        both_logs = tops + jnp.log2(totals)
        logs = both_logs[skip:]
        big = logs.astype(BF16)
        rest = logs - big.astype(F32)
        middle = rest.astype(BF16)
        small = (rest - middle.astype(F32)).astype(BF16)
        extra = jnp.where(
            chunk_lane < SHARED_HEADS,
            big.astype(F32),
            jnp.where(chunk_lane < 2 * SHARED_HEADS, middle.astype(F32), small.astype(F32)),
        )
        ps_buf[step - 1, c, :, channels : channels + EXTRA] = extra.astype(BF16)
        partial_out(c, step).start()
        if with_own:
            for h, values in zip(all_heads, summed):
                ol_buf[pl.ds(first, per_chunk), turn, :, lanes_of(h)] = values[:skip].reshape(
                    per_chunk, ROWS, HEAD_DIM
                )
            ll_buf[pl.ds(first, per_chunk), turn] = both_logs[:skip].reshape(
                per_chunk, ROWS, HEAD_DIM
            )

    def rows_out(group, turn, peer):
        return remote(
            n_buf.at[turn, group],
            x_buf.at[turn, half_count + place],
            a_send.at[turn, group],
            a_recv.at[turn, place],
            "tm",
            half * half_count + peer,
        )

    def rows_later(group, turn, peer):
        return remote(
            n_buf.at[turn, group],
            x_buf.at[turn, place],
            l_send.at[turn, group],
            l_recv.at[turn, place],
            "tm",
            half_count + peer,
        )

    def rows_in(turn, sender):
        return remote(
            n_buf.at[turn, 0],
            x_buf.at[turn, half_count + sender],
            a_send.at[turn, 0],
            a_recv.at[turn, sender],
            "tm",
            half * half_count + sender,
        )

    def earlier_in(turn, sender):
        return remote(
            n_buf.at[turn, 0],
            x_buf.at[turn, sender],
            l_send.at[turn, 0],
            l_recv.at[turn, sender],
            "tm",
            sender,
        )

    def rows_home(turn):
        return pltpu.make_async_copy(
            n_buf.at[turn, place], x_buf.at[turn, half_count + place], self_sem.at[turn]
        )

    def merge(c):
        turn, first = chunk_groups(c)
        loop(1, chips, lambda step: partial_out(c, step).wait_recv())
        logs = [ll_buf[pl.ds(first, per_chunk), turn].reshape(rows, HEAD_DIM)]
        for step in range(1, chips):
            extra = pr_buf[step - 1, c, :, channels : channels + EXTRA].astype(F32)
            once = pltpu.roll(extra, EXTRA - SHARED_HEADS, 1)
            twice = pltpu.roll(extra, EXTRA - 2 * SHARED_HEADS, 1)
            logs.append(extra + (once + twice))
        top = functools.reduce(jnp.maximum, logs)
        shares = [jnp.exp2(log - top) for log in logs]
        total = functools.reduce(jnp.add, shares)
        shares = [share / total for share in shares]
        attended = []
        for h in all_heads:
            value = shares[0][:, h : h + 1] * ol_buf[
                pl.ds(first, per_chunk), turn, :, lanes_of(h)
            ].reshape(rows, HEAD_DIM)
            for step in range(1, chips):
                value = value + shares[step][:, h : h + 1] * pr_buf[
                    step - 1, c, :, lanes_of(h)
                ].astype(F32)
            attended.append(value.astype(BF16).astype(F32))
        squares = functools.reduce(jnp.add, [a * a for a in attended])
        mean = jnp.sum(squares, axis=-1, keepdims=True) / channels
        scale = lax.rsqrt(mean + 1e-05)
        for h in all_heads:
            normed = attended[h] * scale * pre_ref[:, lanes_of(h)]
            n_buf[turn, pl.ds(first, per_chunk), :, lanes_of(h)] = normed.reshape(
                per_chunk, ROWS, HEAD_DIM
            ).astype(BF16)
        for index in range(per_chunk):
            peer = first + index

            @pl.when(peer != place)
            def _():
                rows_out(peer, turn, peer).start()

            @pl.when(peer == place)
            def _():
                rows_home(turn).start()

            @pl.when(half == 0)
            def _():
                rows_later(peer, turn, peer).start()

    def result_out(turn, step):
        peer = lax.rem(place + step, half_count)
        return remote(
            o_buf.at[turn, peer],
            out_ref.at[place, turn],
            o_send.at[turn, step],
            o_recv.at[turn, step],
            "tm",
            half * half_count + peer,
        )

    def result_in(turn, step):
        sender = lax.rem(place - step + half_count, half_count)
        return remote(
            o_buf.at[turn, sender],
            out_ref.at[sender, turn],
            o_send.at[turn, step],
            o_recv.at[turn, step],
            "tm",
            half * half_count + sender,
        )

    def result_home(turn):
        return pltpu.make_async_copy(
            o_buf.at[turn, place], out_ref.at[place, turn], home_sem.at[turn]
        )

    def mix(turn):
        def take(step):
            rows_in(turn, lax.rem(place - step + half_count, half_count)).wait_recv()

        loop(1, half_count, take)
        rows_home(turn).wait()

        @pl.when(half == 1)
        def _():
            loop(0, half_count, lambda sender: earlier_in(turn, sender).wait_recv())

        values = x_buf[turn].reshape(both_rows, channels)
        across = (((1,), (1,)), ((), ()))
        b_in = lax.dot_general(values, w_in_ref[...], across, preferred_element_type=F32)
        c_out = lax.dot_general(
            values[own_rows:], w_out_ref[...], across, preferred_element_type=F32
        )
        gram = lax.dot_general(c_out, b_in, across, precision=HIGH, preferred_element_type=F32)
        mixing = [(gram * d_buf[turn, h]).astype(BF16) for h in all_heads]
        mixed = [
            jnp.dot(m, values[:, lanes_of(h)], preferred_element_type=F32)
            for m, h in zip(mixing, all_heads)
        ]
        mixed = [
            m + skips_ref[h] * values[own_rows:, lanes_of(h)].astype(F32)
            for m, h in zip(mixed, all_heads)
        ]
        squares = functools.reduce(jnp.add, [m * m for m in mixed])
        mean = jnp.sum(squares, axis=-1, keepdims=True) / channels
        scale = lax.rsqrt(mean + 1e-05)
        for h in all_heads:
            result = mixed[h] * scale * post_ref[:, lanes_of(h)]
            o_buf[turn, :, :, lanes_of(h)] = result.reshape(half_count, ROWS, HEAD_DIM).astype(BF16)
        loop(1, half_count, lambda step: result_out(turn, half_count - step).start())
        result_home(turn).start()

    def turn_of_loop(i):
        @pl.when(i < chunks)
        def _():
            attend_for(i, 1, True)
            loop(2, chips, lambda step: attend_for(i, step, False))

        @pl.when(i + ahead < chunks)
        def _():
            send_query(i + ahead)

        @pl.when((i >= lag_merge) & (i < chunks + lag_merge))
        def _():
            merge(i - lag_merge)

        @pl.when(i == 1)
        def _():
            send_steps()

        @pl.when(i == lag_mix - 1)
        def _():
            make_decays()

        c = i - lag_mix
        turn, first = chunk_groups(jnp.maximum(c, 0))

        @pl.when((c >= 0) & (c < chunks) & (place >= first) & (place < first + per_chunk))
        def _():
            mix(turn)

    loop(0, chunks + max(LAG_MIX), turn_of_loop)

    for part in range(KV_PARTS):
        for which in range(2):
            partner_kv(which, part).wait_send()
    for which in range(2):
        target = which * half_count + tm // 2

        @pl.when(target != tm)
        def _():
            step_copy(which, target, tm % 2).wait_send()

    def sent_chunk(c):
        def sent(step):
            query_out(c, step).wait_send()
            partial_out(c, step).wait_send()

        loop(1, chips, sent)

    loop(0, chunks, sent_chunk)

    for turn in range(turns):

        def sent_rows(group):
            @pl.when(half == 0)
            def _():
                rows_later(group, turn, group).wait_send()

            @pl.when(group != place)
            def _():
                rows_out(group, turn, group).wait_send()

        loop(0, half_count, sent_rows)

    for turn in range(turns):

        def finish(step):
            result_out(turn, step).wait_send()
            result_in(turn, step).wait_recv()

        loop(1, half_count, finish)
        result_home(turn).wait()


def body(
    queries,
    key_vectors,
    value_vectors,
    block_lists,
    step_sizes,
    decay_rates,
    skip_gains,
    pre_gain,
    state_in_weight,
    state_out_weight,
    post_gain,
):
    tokens, channels = queries.shape[1], queries.shape[2]
    space_count = lax.axis_size("space")
    tm_count = lax.axis_size("tm")
    half_count = tm_count // 2
    turns = tokens // (half_count * ROWS)
    chips = space_count // 2
    chunks = half_count * turns // PER_CHUNK
    rows = PER_CHUNK * ROWS
    state = state_in_weight.shape[1]
    hbm = pl.BlockSpec(memory_space=pl.ANY)
    dma = pltpu.SemaphoreType.DMA
    out = pl.pallas_call(
        functools.partial(kernel, (space_count, tm_count, block_lists.shape[1])),
        out_shape=jax.ShapeDtypeStruct((half_count, turns, ROWS, channels), BF16),
        in_specs=[hbm] * 11,
        out_specs=hbm,
        scratch_shapes=[
            pltpu.SMEM(block_lists.shape, jnp.int32),
            pltpu.SMEM(decay_rates.shape, F32),
            pltpu.SMEM(skip_gains.shape, F32),
            pltpu.VMEM((half_count, turns, ROWS, channels), BF16),
            pltpu.VMEM((tm_count, 2, tokens // tm_count, SHARED_HEADS), F32),
            pltpu.VMEM((1, channels), F32),
            pltpu.VMEM((state, channels), BF16),
            pltpu.VMEM((state, channels), BF16),
            pltpu.VMEM((1, channels), F32),
            pltpu.VMEM((2, 2, tokens, channels), BF16),
            pltpu.VMEM((chips - 1, chunks, PER_CHUNK, ROWS, channels), BF16),
            pltpu.VMEM((chips - 1, chunks, rows, channels + EXTRA), BF16),
            pltpu.VMEM((chips - 1, chunks, rows, channels + EXTRA), BF16),
            pltpu.VMEM((half_count, turns, ROWS, channels), F32),
            pltpu.VMEM((half_count, turns, ROWS, HEAD_DIM), F32),
            pltpu.VMEM((turns, half_count, ROWS, channels), BF16),
            pltpu.VMEM((turns, tm_count, ROWS, channels), BF16),
            pltpu.VMEM((turns, half_count, ROWS, channels), BF16),
            pltpu.VMEM((turns, SHARED_HEADS, half_count * ROWS, tm_count * ROWS), F32),
            dma((8,)),
            dma((2, KV_PARTS)),
            dma((2, KV_PARTS)),
            dma((2, KV_PARTS)),
            dma((2,)),
            dma((2,)),
            dma((2,)),
            dma((chips - 1, chunks)),
            dma((chips - 1, chunks)),
            dma((chips - 1, chunks)),
            dma((chips - 1, chunks)),
            dma((turns, half_count)),
            dma((turns, half_count)),
            dma((turns, half_count)),
            dma((turns, half_count)),
            dma((turns, half_count)),
            dma((turns, half_count)),
            dma((turns,)),
            dma((turns,)),
            pltpu.SemaphoreType.REGULAR,
        ],
        compiler_params=pltpu.CompilerParams(
            collective_id=0, has_side_effects=True, vmem_limit_bytes=VMEM_BYTES
        ),
        name="attend_and_mix",
    )(
        *(
            pltpu.with_memory_space_constraint(operand, pltpu.HBM)
            for operand in (
                block_lists,
                decay_rates,
                skip_gains,
                queries.reshape(half_count, turns, ROWS, channels),
                key_vectors.reshape(tokens, channels),
                value_vectors.reshape(tokens, channels),
                step_sizes,
                pre_gain.reshape(1, channels),
                state_in_weight.T,
                state_out_weight.T,
                post_gain.reshape(1, channels),
            )
        )
    )
    return out.reshape(1, tokens, channels)


def solution(mesh):
    placed = (
        P("tm", "space", None),
        P("tm", "space", None),
        P("tm", "space", None),
        P(),
        P(None, ("space", "tm"), None),
        P(),
        P(),
        P(),
        P(),
        P(),
        P(),
    )
    return jax.shard_map(
        body, mesh=mesh, in_specs=placed, out_specs=P("tm", "space", None), check_vma=False
    )
```

```python
import functools
import math

import jax
import jax.numpy as jnp
from jax import lax
from jax.experimental import pallas as pl
from jax.experimental.pallas import tpu as pltpu
from jax.sharding import PartitionSpec as P

SHARED_HEADS = 16
HEAD_DIM = 128
ROWS = 8
PER_CHUNK = 1
AHEAD = (5, 5)
LAG_MERGE = (4, 3)
LAG_MIX = (7, 6)
KV_PARTS = 1
EXTRA = 128
VMEM_BYTES = 44 * 1024 * 1024
MESH = pl.DeviceIdType.MESH
F32 = jnp.float32
BF16 = jnp.bfloat16
HIGH = lax.Precision.HIGHEST


def remote(src, dst, send_sem, recv_sem, axis, index):
    return pltpu.make_async_remote_copy(
        src_ref=src,
        dst_ref=dst,
        send_sem=send_sem,
        recv_sem=recv_sem,
        device_id={axis: index},
        device_id_type=MESH,
    )


def loop(low, high, act):
    if high - low == 1:
        act(low)
    elif high > low:

        def turn(i, carry):
            act(i)
            return carry

        lax.fori_loop(low, high, turn, 0)


def lanes_of(head):
    return slice(head * HEAD_DIM, (head + 1) * HEAD_DIM)


def attend(query, key, value, bias, heads):
    factor = math.log2(math.e) / math.sqrt(HEAD_DIM)
    across = (((1,), (1,)), ((), ()))
    scores = [
        lax.dot_general(query(h), key(h), across, preferred_element_type=F32) * factor + bias
        for h in heads
    ]
    tops = [jnp.max(s, axis=-1, keepdims=True) for s in scores]
    weights = [jnp.exp2(s - m) for s, m in zip(scores, tops)]
    totals = [jnp.sum(w, axis=-1, keepdims=True) for w in weights]
    sums = [
        jnp.dot(w.astype(BF16), value(h), preferred_element_type=F32) for w, h in zip(weights, heads)
    ]
    return [s / t for s, t in zip(sums, totals)], tops, totals


def packed(columns, heads, lane, into):
    for h, column in zip(heads, columns):
        into = jnp.where(lane == h, column, into)
    return into


def kernel(
    dims,
    lists_hbm,
    rates_hbm,
    skips_hbm,
    q_hbm,
    k_hbm,
    v_hbm,
    steps_hbm,
    pre_hbm,
    w_in_hbm,
    w_out_hbm,
    post_hbm,
    out_ref,
    lists_ref,
    rates_ref,
    skips_ref,
    q_ref,
    steps_ref,
    pre_ref,
    w_in_ref,
    w_out_ref,
    post_ref,
    kv_buf,
    qr_buf,
    ps_buf,
    pr_buf,
    ol_buf,
    ll_buf,
    n_buf,
    x_buf,
    o_buf,
    d_buf,
    load_sem,
    own_sem,
    kv_send,
    kv_recv,
    step_send,
    step_recv,
    step_own,
    q_send,
    q_recv,
    p_send,
    p_recv,
    a_send,
    a_recv,
    l_send,
    l_recv,
    o_send,
    o_recv,
    self_sem,
    home_sem,
    ready_sem,
):
    space_count, tm_count, list_width = dims
    half_count, turns, _, channels = q_hbm.shape
    tokens = half_count * turns * ROWS
    per_chunk = PER_CHUNK
    sets = half_count // per_chunk
    chunks = sets * turns
    rows = per_chunk * ROWS
    chips = space_count // 2
    all_heads = range(SHARED_HEADS)
    space = lax.axis_index("space")
    tm = lax.axis_index("tm")
    half = tm // half_count
    place = tm % half_count
    chip = space // 2
    core = space % 2
    partner = chip * 2 + 1 - core
    ahead, lag_merge, lag_mix = (
        pair[1] + (1 - core) * (pair[0] - pair[1]) for pair in (AHEAD, LAG_MERGE, LAG_MIX)
    )

    barrier = pltpu.get_barrier_semaphore()

    def greet_chip(step):
        peer = lax.rem(chip + step, chips) * 2 + 1 - core
        pl.semaphore_signal(barrier, inc=1, device_id={"space": peer}, device_id_type=MESH)

    def greet_frame(peer):
        pl.semaphore_signal(barrier, inc=1, device_id={"tm": peer}, device_id_type=MESH)

    def answer_frame(peer):
        pl.semaphore_signal(ready_sem, inc=1, device_id={"tm": peer}, device_id_type=MESH)

    pl.semaphore_signal(barrier, inc=1, device_id={"space": partner}, device_id_type=MESH)
    loop(1, chips, greet_chip)
    lax.fori_loop(tm + 1, tm_count, lambda peer, carry: (greet_frame(peer), carry)[1], 0)

    part_width = channels // KV_PARTS

    def kv_span(part):
        return pl.ds(part * part_width, part_width)

    def own_kv(which, part):
        source = (k_hbm, v_hbm)[which]
        return pltpu.make_async_copy(
            source.at[:, kv_span(part)],
            kv_buf.at[which, core, :, kv_span(part)],
            own_sem.at[which, part],
        )

    def partner_kv(which, part):
        source = (k_hbm, v_hbm)[which]
        return remote(
            source.at[:, kv_span(part)],
            kv_buf.at[which, core, :, kv_span(part)],
            kv_send.at[which, part],
            kv_recv.at[which, part],
            "space",
            partner,
        )

    load_q = pltpu.make_async_copy(q_hbm, q_ref, load_sem.at[0])
    load_q.start()
    for part in range(KV_PARTS):
        for which in range(2):
            own_kv(which, part).start()
    loads = [
        pltpu.make_async_copy(source, target, load_sem.at[1 + index])
        for index, (source, target) in enumerate(
            (
                (lists_hbm, lists_ref),
                (rates_hbm, rates_ref),
                (skips_hbm, skips_ref),
                (pre_hbm, pre_ref),
                (w_in_hbm, w_in_ref),
                (w_out_hbm, w_out_ref),
                (post_hbm, post_ref),
            )
        )
    ]
    for load in loads:
        load.start()

    def chunk_groups(c):
        return c // sets, (sets - 1 - c % sets) * per_chunk

    def query_out(c, step):
        turn, first = chunk_groups(c)
        return remote(
            q_hbm.at[pl.ds(first, per_chunk), turn],
            qr_buf.at[step - 1, c],
            q_send.at[step - 1, c],
            q_recv.at[step - 1, c],
            "space",
            lax.rem(chip + step, chips) * 2 + 1 - core,
        )

    def partial_out(c, step):
        return remote(
            ps_buf.at[step - 1, c],
            pr_buf.at[step - 1, c],
            p_send.at[step - 1, c],
            p_recv.at[step - 1, c],
            "space",
            lax.rem(chip - step + chips, chips) * 2 + 1 - core,
        )

    def send_query(c):
        loop(1, chips, lambda step: query_out(c, step).start())

    pl.semaphore_wait(barrier, chips + tm)

    send_query(0)
    for part in range(KV_PARTS):
        for which in range(2):
            partner_kv(which, part).start()
    lax.fori_loop(1, jnp.minimum(ahead, chunks), lambda c, carry: (send_query(c), carry)[1], 0)
    lax.fori_loop(0, tm, lambda peer, carry: (answer_frame(peer), carry)[1], 0)

    def step_copy(which, target, part):
        return remote(
            steps_hbm,
            steps_ref.at[:, part],
            step_send.at[which],
            step_recv.at[part],
            "tm",
            target,
        )

    def step_local(part):
        return pltpu.make_async_copy(steps_hbm, steps_ref.at[:, part], step_own.at[part])

    for load in loads:
        load.wait()
    load_q.wait()

    def key_of(h):
        return kv_buf[0, :, :, lanes_of(h)].reshape(2 * tokens, HEAD_DIM)

    def value_of(h):
        return kv_buf[1, :, :, lanes_of(h)].reshape(2 * tokens, HEAD_DIM)

    block_of = chip * 2 + lax.broadcasted_iota(jnp.int32, (1, 2 * tokens), 1) // tokens

    def bias_of(owner):
        chosen = block_of == lists_ref[owner, 0]
        for entry in range(1, list_width):
            chosen = chosen | (block_of == lists_ref[owner, entry])
        return jnp.where(chosen, 0.0, -1e30).astype(F32)

    own_rows = half_count * ROWS
    both_rows = tm_count * ROWS

    def send_steps():
        @pl.when(tm < tm_count - 1)
        def _():
            pl.semaphore_wait(ready_sem, tm_count - 1 - tm)

        for which in range(2):
            target = which * half_count + tm // 2
            part = tm % 2

            @pl.when(target != tm)
            def _():
                step_copy(which, target, part).start()

            @pl.when(target == tm)
            def _():
                step_local(part).start()

    def make_decays():
        for part in range(2):
            origin = 2 * place + part

            @pl.when(origin != tm)
            def _():
                step_copy(0, origin, part).wait_recv()

            @pl.when(origin == tm)
            def _():
                step_local(part).wait()

        steps = steps_ref[...].reshape(tm_count, turns, ROWS, SHARED_HEADS)
        earlier, later = steps[:half_count], steps[half_count:]
        own = jnp.where(half == 1, later, earlier)
        steps = jnp.concatenate([earlier, own], axis=0)
        counted = jnp.concatenate([jnp.where(half == 1, earlier, 0.0), own], axis=0)
        run = [counted[0]]
        for frame in range(1, tm_count):
            run.append(run[-1] + counted[frame])
        run = jnp.stack(run)
        row = half_count * ROWS + lax.broadcasted_iota(jnp.int32, (own_rows, both_rows), 0)
        col = lax.broadcasted_iota(jnp.int32, (own_rows, both_rows), 1)
        counts = (row % ROWS == col % ROWS) & (col // ROWS <= row // ROWS)
        counts = counts & (col >= (1 - half) * own_rows)
        for turn in range(turns):
            total = run[:, turn].reshape(both_rows, SHARED_HEADS)
            total_t = jnp.transpose(total)
            steps_t = jnp.transpose(steps[:, turn].reshape(both_rows, SHARED_HEADS))
            for head in all_heads:
                gap = total_t[head : head + 1, :] - total[own_rows:, head : head + 1]
                decay = jnp.exp(jnp.where(counts, gap * rates_ref[head], -1e30))
                d_buf[turn, head] = decay * steps_t[head : head + 1, :]

    for part in range(KV_PARTS):
        for which in range(2):
            own_kv(which, part).wait()
            partner_kv(which, part).wait_recv()

    @pl.when(half == 0)
    def _():
        x_buf[:, 0:half_count] = jnp.zeros((turns, half_count, ROWS, channels), BF16)

    chunk_lane = lax.broadcasted_iota(jnp.int32, (rows, HEAD_DIM), 1)

    def attend_for(c, step, with_own):
        turn, first = chunk_groups(c)
        query_out(c, step).wait_recv()
        owner = lax.rem(chip - step + chips, chips) * 2 + 1 - core
        query = qr_buf[step - 1, c].reshape(rows, channels)
        bias = bias_of(owner)
        skip = rows if with_own else 0
        if with_own:
            mine = q_ref[pl.ds(first, per_chunk), turn].reshape(rows, channels)
            query = jnp.concatenate([mine.astype(F32), query.astype(F32)], axis=0).astype(BF16)
            row_of = lax.broadcasted_iota(jnp.int32, (2 * rows, 2 * tokens), 0)
            bias = jnp.where(row_of < rows, bias_of(space), bias)
        summed, top, total = attend(
            lambda h: query[:, lanes_of(h)], key_of, value_of, bias, all_heads
        )
        slot_of = lax.broadcasted_iota(jnp.int32, (skip + rows, HEAD_DIM), 1) % SHARED_HEADS
        for h, values in zip(all_heads, summed):
            ps_buf[step - 1, c, :, lanes_of(h)] = values[skip:].astype(BF16)
        tops = packed(top, all_heads, slot_of, jnp.zeros((skip + rows, HEAD_DIM), F32))
        totals = packed(total, all_heads, slot_of, jnp.ones((skip + rows, HEAD_DIM), F32))
        both_logs = tops + jnp.log2(totals)
        logs = both_logs[skip:]
        big = logs.astype(BF16)
        rest = logs - big.astype(F32)
        middle = rest.astype(BF16)
        small = (rest - middle.astype(F32)).astype(BF16)
        extra = jnp.where(
            chunk_lane < SHARED_HEADS,
            big.astype(F32),
            jnp.where(chunk_lane < 2 * SHARED_HEADS, middle.astype(F32), small.astype(F32)),
        )
        ps_buf[step - 1, c, :, channels : channels + EXTRA] = extra.astype(BF16)
        partial_out(c, step).start()
        if with_own:
            for h, values in zip(all_heads, summed):
                ol_buf[pl.ds(first, per_chunk), turn, :, lanes_of(h)] = values[:skip].reshape(
                    per_chunk, ROWS, HEAD_DIM
                )
            ll_buf[pl.ds(first, per_chunk), turn] = both_logs[:skip].reshape(
                per_chunk, ROWS, HEAD_DIM
            )

    def rows_out(group, turn, peer):
        return remote(
            n_buf.at[turn, group],
            x_buf.at[turn, half_count + place],
            a_send.at[turn, group],
            a_recv.at[turn, place],
            "tm",
            half * half_count + peer,
        )

    def rows_later(group, turn, peer):
        return remote(
            n_buf.at[turn, group],
            x_buf.at[turn, place],
            l_send.at[turn, group],
            l_recv.at[turn, place],
            "tm",
            half_count + peer,
        )

    def rows_in(turn, sender):
        return remote(
            n_buf.at[turn, 0],
            x_buf.at[turn, half_count + sender],
            a_send.at[turn, 0],
            a_recv.at[turn, sender],
            "tm",
            half * half_count + sender,
        )

    def earlier_in(turn, sender):
        return remote(
            n_buf.at[turn, 0],
            x_buf.at[turn, sender],
            l_send.at[turn, 0],
            l_recv.at[turn, sender],
            "tm",
            sender,
        )

    def rows_home(turn):
        return pltpu.make_async_copy(
            n_buf.at[turn, place], x_buf.at[turn, half_count + place], self_sem.at[turn]
        )

    def merge(c):
        turn, first = chunk_groups(c)
        loop(1, chips, lambda step: partial_out(c, step).wait_recv())
        logs = [ll_buf[pl.ds(first, per_chunk), turn].reshape(rows, HEAD_DIM)]
        for step in range(1, chips):
            extra = pr_buf[step - 1, c, :, channels : channels + EXTRA].astype(F32)
            once = pltpu.roll(extra, EXTRA - SHARED_HEADS, 1)
            twice = pltpu.roll(extra, EXTRA - 2 * SHARED_HEADS, 1)
            logs.append(extra + (once + twice))
        top = functools.reduce(jnp.maximum, logs)
        shares = [jnp.exp2(log - top) for log in logs]
        total = functools.reduce(jnp.add, shares)
        shares = [share / total for share in shares]
        attended = []
        for h in all_heads:
            value = shares[0][:, h : h + 1] * ol_buf[
                pl.ds(first, per_chunk), turn, :, lanes_of(h)
            ].reshape(rows, HEAD_DIM)
            for step in range(1, chips):
                value = value + shares[step][:, h : h + 1] * pr_buf[
                    step - 1, c, :, lanes_of(h)
                ].astype(F32)
            attended.append(value.astype(BF16).astype(F32))
        squares = functools.reduce(jnp.add, [a * a for a in attended])
        mean = jnp.sum(squares, axis=-1, keepdims=True) / channels
        scale = lax.rsqrt(mean + 1e-05)
        for h in all_heads:
            normed = attended[h] * scale * pre_ref[:, lanes_of(h)]
            n_buf[turn, pl.ds(first, per_chunk), :, lanes_of(h)] = normed.reshape(
                per_chunk, ROWS, HEAD_DIM
            ).astype(BF16)
        for index in range(per_chunk):
            peer = first + index

            @pl.when(half == 0)
            def _():
                rows_later(peer, turn, peer).start()

            @pl.when(peer != place)
            def _():
                rows_out(peer, turn, peer).start()

            @pl.when(peer == place)
            def _():
                rows_home(turn).start()

    def result_out(turn, step):
        peer = lax.rem(place + step, half_count)
        return remote(
            o_buf.at[turn, peer],
            out_ref.at[place, turn],
            o_send.at[turn, step],
            o_recv.at[turn, step],
            "tm",
            half * half_count + peer,
        )

    def result_in(turn, step):
        sender = lax.rem(place - step + half_count, half_count)
        return remote(
            o_buf.at[turn, sender],
            out_ref.at[sender, turn],
            o_send.at[turn, step],
            o_recv.at[turn, step],
            "tm",
            half * half_count + sender,
        )

    def result_home(turn):
        return pltpu.make_async_copy(
            o_buf.at[turn, place], out_ref.at[place, turn], home_sem.at[turn]
        )

    def mix(turn):
        def take(step):
            rows_in(turn, lax.rem(place - step + half_count, half_count)).wait_recv()

        loop(1, half_count, take)
        rows_home(turn).wait()

        @pl.when(half == 1)
        def _():
            loop(0, half_count, lambda sender: earlier_in(turn, sender).wait_recv())

        values = x_buf[turn].reshape(both_rows, channels)
        across = (((1,), (1,)), ((), ()))
        b_in = lax.dot_general(values, w_in_ref[...], across, preferred_element_type=F32)
        c_out = lax.dot_general(
            values[own_rows:], w_out_ref[...], across, preferred_element_type=F32
        )
        gram = lax.dot_general(c_out, b_in, across, precision=HIGH, preferred_element_type=F32)
        mixing = [(gram * d_buf[turn, h]).astype(BF16) for h in all_heads]
        mixed = [
            jnp.dot(m, values[:, lanes_of(h)], preferred_element_type=F32)
            for m, h in zip(mixing, all_heads)
        ]
        mixed = [
            m + skips_ref[h] * values[own_rows:, lanes_of(h)].astype(F32)
            for m, h in zip(mixed, all_heads)
        ]
        squares = functools.reduce(jnp.add, [m * m for m in mixed])
        mean = jnp.sum(squares, axis=-1, keepdims=True) / channels
        scale = lax.rsqrt(mean + 1e-05)
        for h in all_heads:
            result = mixed[h] * scale * post_ref[:, lanes_of(h)]
            o_buf[turn, :, :, lanes_of(h)] = result.reshape(half_count, ROWS, HEAD_DIM).astype(BF16)
        loop(1, half_count, lambda step: result_out(turn, half_count - step).start())
        result_home(turn).start()

    def turn_of_loop(i):
        @pl.when(i < chunks)
        def _():
            attend_for(i, 1, True)
            loop(2, chips, lambda step: attend_for(i, step, False))

        @pl.when(i + ahead < chunks)
        def _():
            send_query(i + ahead)

        @pl.when((i >= lag_merge) & (i < chunks + lag_merge))
        def _():
            merge(i - lag_merge)

        @pl.when(i == 1)
        def _():
            send_steps()

        @pl.when(i == lag_mix - 1)
        def _():
            make_decays()

        c = i - lag_mix
        turn, first = chunk_groups(jnp.maximum(c, 0))

        @pl.when((c >= 0) & (c < chunks) & (place >= first) & (place < first + per_chunk))
        def _():
            mix(turn)

    loop(0, chunks + max(LAG_MIX), turn_of_loop)

    for part in range(KV_PARTS):
        for which in range(2):
            partner_kv(which, part).wait_send()
    for which in range(2):
        target = which * half_count + tm // 2

        @pl.when(target != tm)
        def _():
            step_copy(which, target, tm % 2).wait_send()

    def sent_chunk(c):
        def sent(step):
            query_out(c, step).wait_send()
            partial_out(c, step).wait_send()

        loop(1, chips, sent)

    loop(0, chunks, sent_chunk)

    for turn in range(turns):

        def sent_rows(group):
            @pl.when(half == 0)
            def _():
                rows_later(group, turn, group).wait_send()

            @pl.when(group != place)
            def _():
                rows_out(group, turn, group).wait_send()

        loop(0, half_count, sent_rows)

    for turn in range(turns):

        def finish(step):
            result_out(turn, step).wait_send()
            result_in(turn, step).wait_recv()

        loop(1, half_count, finish)
        result_home(turn).wait()


def body(
    queries,
    key_vectors,
    value_vectors,
    block_lists,
    step_sizes,
    decay_rates,
    skip_gains,
    pre_gain,
    state_in_weight,
    state_out_weight,
    post_gain,
):
    tokens, channels = queries.shape[1], queries.shape[2]
    space_count = lax.axis_size("space")
    tm_count = lax.axis_size("tm")
    half_count = tm_count // 2
    turns = tokens // (half_count * ROWS)
    chips = space_count // 2
    chunks = half_count * turns // PER_CHUNK
    rows = PER_CHUNK * ROWS
    state = state_in_weight.shape[1]
    hbm = pl.BlockSpec(memory_space=pl.ANY)
    dma = pltpu.SemaphoreType.DMA
    out = pl.pallas_call(
        functools.partial(kernel, (space_count, tm_count, block_lists.shape[1])),
        out_shape=jax.ShapeDtypeStruct((half_count, turns, ROWS, channels), BF16),
        in_specs=[hbm] * 11,
        out_specs=hbm,
        scratch_shapes=[
            pltpu.SMEM(block_lists.shape, jnp.int32),
            pltpu.SMEM(decay_rates.shape, F32),
            pltpu.SMEM(skip_gains.shape, F32),
            pltpu.VMEM((half_count, turns, ROWS, channels), BF16),
            pltpu.VMEM((tm_count, 2, tokens // tm_count, SHARED_HEADS), F32),
            pltpu.VMEM((1, channels), F32),
            pltpu.VMEM((state, channels), BF16),
            pltpu.VMEM((state, channels), BF16),
            pltpu.VMEM((1, channels), F32),
            pltpu.VMEM((2, 2, tokens, channels), BF16),
            pltpu.VMEM((chips - 1, chunks, PER_CHUNK, ROWS, channels), BF16),
            pltpu.VMEM((chips - 1, chunks, rows, channels + EXTRA), BF16),
            pltpu.VMEM((chips - 1, chunks, rows, channels + EXTRA), BF16),
            pltpu.VMEM((half_count, turns, ROWS, channels), F32),
            pltpu.VMEM((half_count, turns, ROWS, HEAD_DIM), F32),
            pltpu.VMEM((turns, half_count, ROWS, channels), BF16),
            pltpu.VMEM((turns, tm_count, ROWS, channels), BF16),
            pltpu.VMEM((turns, half_count, ROWS, channels), BF16),
            pltpu.VMEM((turns, SHARED_HEADS, half_count * ROWS, tm_count * ROWS), F32),
            dma((8,)),
            dma((2, KV_PARTS)),
            dma((2, KV_PARTS)),
            dma((2, KV_PARTS)),
            dma((2,)),
            dma((2,)),
            dma((2,)),
            dma((chips - 1, chunks)),
            dma((chips - 1, chunks)),
            dma((chips - 1, chunks)),
            dma((chips - 1, chunks)),
            dma((turns, half_count)),
            dma((turns, half_count)),
            dma((turns, half_count)),
            dma((turns, half_count)),
            dma((turns, half_count)),
            dma((turns, half_count)),
            dma((turns,)),
            dma((turns,)),
            pltpu.SemaphoreType.REGULAR,
        ],
        compiler_params=pltpu.CompilerParams(
            collective_id=0, has_side_effects=True, vmem_limit_bytes=VMEM_BYTES
        ),
        name="attend_and_mix",
    )(
        *(
            pltpu.with_memory_space_constraint(operand, pltpu.HBM)
            for operand in (
                block_lists,
                decay_rates,
                skip_gains,
                queries.reshape(half_count, turns, ROWS, channels),
                key_vectors.reshape(tokens, channels),
                value_vectors.reshape(tokens, channels),
                step_sizes,
                pre_gain.reshape(1, channels),
                state_in_weight.T,
                state_out_weight.T,
                post_gain.reshape(1, channels),
            )
        )
    )
    return out.reshape(1, tokens, channels)


def solution(mesh):
    placed = (
        P("tm", "space", None),
        P("tm", "space", None),
        P("tm", "space", None),
        P(),
        P(None, ("space", "tm"), None),
        P(),
        P(),
        P(),
        P(),
        P(),
        P(),
    )
    return jax.shard_map(
        body, mesh=mesh, in_specs=placed, out_specs=P("tm", "space", None), check_vma=False
    )
```
